128 devices in a mesh: dp: 4 (over y_hi, core), mp: 32 (over x, z, y_lo).
Axes of the slice: x: 4, y: 4 (y_hi: 2, y_lo: 2; y = y_hi * 2 + y_lo), z: 4, core: 2. Of those that a mesh axis runs over, the one named last changes fastest.
Arguments:
- step_ids: int32 [32, 4], P('dp'), may hold values from 0 to 31999
- prompt_lens: int32 [32], P('dp'), may hold values from 128 to 1024
- embed_table: bfloat16 [32000, 4096], P(None, 'mp'), may hold values from -170 to 170
- attn_gain: bfloat16 [4096], replicated, may hold values from 0.099609375 to 1.8984375
- w_qkv: bfloat16 [3, 4096, 4096], P(None, None, 'mp'), may hold values from -0.09375 to 0.09375
- w_out: bfloat16 [4096, 4096], P('mp'), may hold values from -0.1875 to 0.1875
- key_cache: bfloat16 [32, 32, 1024, 128], P('dp', 'mp'), may hold values from -194 to 194
- value_cache: bfloat16 [32, 32, 1024, 128], P('dp', 'mp'), may hold values from -6 to 6
- reward_pieces: bfloat16 [32, 4096, 4096], P('dp', None, 'mp'), may hold values from -170 to 170
- piece_lens: int32 [32], P('dp'), may hold values from 256 to 4096
- reward_gain: bfloat16 [4096], replicated, may hold values from 0.099609375 to 1.8984375
- w_value: bfloat16 [4096, 2048], P('mp'), may hold values from -0.09375 to 0.09375
- b_value: float32 [2048], replicated, may hold values from -4 to 4
- w_score: float32 [2048], replicated, may hold values from -0.125 to 0.125
- b_score: float32 [1], replicated, may hold values from -3 to 3
Outputs:
- attn_out: bfloat16 [32, 4, 4096], P('dp')
- piece_values: float32 [32, 4096], P('dp', 'mp')
The draws below stay inside these ranges and needn't reach their ends.
All inputs are finite; a program needn't handle non-finite values.
Results may differ from the reference program's by a relative error of at most 0.015.
Values may be sent and summed in bfloat16 or wider, within the bound.
No kernel may reach another device: no remote copies, remote signals or barrier semaphores. Data moves between devices by JAX's collectives and lax.ppermute only.
A program may use at most 192 MiB of HBM per device.

```python
import math
import jax
import jax.numpy as jnp
from jax import lax

D = 4096
HEADS = 32
HD = 128
VOCAB = 32000
VH = 2048
STEPS = 4
CACHE_LEN = 1024
SEQ = 4096
ROWS = 32
PIECES = 32


def draw_embed_table(key, part):
    col_key, val_key = jax.random.split(jax.random.fold_in(key, 11), 2)
    column_scale = jnp.exp(jax.random.uniform(col_key, (1, D), jnp.float32, 0.0, math.log(10.0)))
    base_values = jnp.clip(jax.random.normal(val_key, (VOCAB, D), jnp.float32), -4.0, 4.0)
    return (base_values * column_scale).astype(jnp.bfloat16)


def draw_reward_pieces(key, part):
    col_key, val_key = jax.random.split(jax.random.fold_in(key, 23), 2)
    column_scale = jnp.exp(jax.random.uniform(col_key, (1, 1, D), jnp.float32, 0.0, math.log(10.0)))
    base_values = jnp.clip(jax.random.normal(val_key, (PIECES, SEQ, D), jnp.float32), -4.0, 4.0)
    return (base_values * column_scale).astype(jnp.bfloat16)


def draw_key_cache(key, part):
    base_key = jax.random.fold_in(jax.random.fold_in(key, 37), 0)
    base_values = jax.random.normal(base_key, (ROWS, HEADS, CACHE_LEN, HD), jnp.float32) * 1.5
    return jnp.clip(base_values, -6.0, 6.0).astype(jnp.bfloat16)


def draw_prompt_lens(key, part):
    len_key, order_key = jax.random.split(jax.random.fold_in(key, 41), 2)
    lengths = jax.random.randint(len_key, (ROWS,), CACHE_LEN // 8, CACHE_LEN + 1)
    ordering = jax.random.permutation(order_key, ROWS)
    return lengths.at[ordering[0]].set(CACHE_LEN).at[ordering[1]].set(CACHE_LEN // 8)


def draw_piece_lens(key, part):
    len_key, order_key = jax.random.split(jax.random.fold_in(key, 53), 2)
    lengths = jax.random.randint(len_key, (PIECES,), SEQ // 16, SEQ + 1)
    ordering = jax.random.permutation(order_key, PIECES)
    return lengths.at[ordering[0]].set(SEQ).at[ordering[1]].set(SEQ // 16)


def with_ends(values, stream_key, least, largest):
    longest = values.shape.index(max(values.shape))
    spots = []
    for shift in (0, 1):
        where = [jax.random.randint(jax.random.fold_in(stream_key, axis), (), 0, length) for axis, length in enumerate(values.shape)]
        where[longest] = (where[longest] + shift) % values.shape[longest]
        spots.append(tuple(where))
    return values.at[spots[0]].set(least).at[spots[1]].set(largest)


def spiked(values, own_key, source, target, shards_of, factor):
    def block_of(axis_at):
        return (jnp.arange(values.shape[axis_at]) // (values.shape[axis_at] // shards_of)).reshape((-1,) + (1,) * (values.ndim - 1 - axis_at))

    one_side = jax.random.permutation(own_key, shards_of)[block_of(target)]
    other_side = (block_of(target) + shards_of // 2) % shards_of
    return jnp.where((block_of(source) == one_side) | (block_of(source) == other_side), factor * values, values)


def block_levels(key, extent, cuts, low, largest):
    def one(dim, blocks):
        heights = jax.random.uniform(jax.random.fold_in(jax.random.fold_in(key, 6), dim), (blocks,), jnp.float32, low / len(cuts), largest / len(cuts))
        return jnp.repeat(jnp.exp(heights), extent[dim] // blocks).reshape((-1,) + (1,) * (len(extent) - dim - 1))

    factor_of = one(*cuts[0])
    for cut in cuts[1:]:
        factor_of = factor_of * one(*cut)
    return factor_of


def normal_values(stream_key, extent, scale, most, shards=(), kind=jnp.bfloat16):
    result = jax.random.normal(stream_key, extent, jnp.float32) * scale
    if len(shards) > 0:
        result = block_levels(stream_key, extent, shards, -0.22, 0.18) * result
    return jnp.clip(result, min=-most, max=most).astype(kind)


def bell_draw_with(key, shape, deviation, bound, shards, heavy, kind=jnp.bfloat16):
    drawn = deviation * jax.random.normal(key, shape, jnp.float32)
    if shards:
        drawn = drawn * block_levels(key, shape, shards, -0.22, 0.18)
    return jnp.clip(spiked(drawn, jax.random.fold_in(key, 3), *heavy), -bound, bound).astype(kind)


def setup_inputs(seed: int = 0) -> dict:
    seeds = jax.random.split(jax.random.key(seed), 16)
    return {
        "step_ids": with_ends(jax.random.randint(seeds[0], (ROWS, STEPS), 0, VOCAB), jax.random.fold_in(seeds[0], 1), 0, VOCAB - 1).astype(jnp.int32),
        "prompt_lens": draw_prompt_lens(jax.random.fold_in(seeds[15], 71), 0),
        "embed_table": draw_embed_table(jax.random.fold_in(seeds[15], 71), 0),
        "attn_gain": jnp.clip(1.0 + 0.18 * jax.random.normal(seeds[3], (D,), jnp.float32), 0.099609375, 1.8984375).astype(jnp.bfloat16),
        "w_qkv": normal_values(seeds[4], (3, D, D), D ** -0.5, 0.09375, ((2, 32),)),
        "w_out": bell_draw_with(seeds[5], (D, D), D ** -0.5, 0.1875, ((0, 32),), (0, 1, 32, 2.75)),
        "key_cache": draw_key_cache(jax.random.fold_in(seeds[15], 71), 0),
        "value_cache": normal_values(seeds[7], (ROWS, HEADS, CACHE_LEN, HD), 1.0, 6.0, ((0, 4), (1, 32))),
        "reward_pieces": draw_reward_pieces(jax.random.fold_in(seeds[15], 71), 0),
        "piece_lens": draw_piece_lens(jax.random.fold_in(seeds[15], 71), 0),
        "reward_gain": jnp.clip(1.0 + 0.18 * jax.random.normal(seeds[10], (D,), jnp.float32), 0.099609375, 1.8984375).astype(jnp.bfloat16),
        "w_value": normal_values(seeds[11], (D, VH), D ** -0.5, 0.09375, ((0, 32),)),
        "b_value": normal_values(seeds[12], (VH,), 1.0, 4.0, (), jnp.float32),
        "w_score": normal_values(seeds[13], (VH,), VH ** -0.5, 0.125, (), jnp.float32),
        "b_score": normal_values(seeds[14], (1,), 1.0, 3.0, (), jnp.float32),
    }


epsilon = 1e-05
masked = -1e+30

def normalize(rows_in, gain_vec):
    widened = rows_in.astype(jnp.float32)
    inverse_rms = lax.rsqrt(lax.optimization_barrier(jnp.mean(widened * widened, axis=-1, keepdims=True)) + epsilon)
    return (widened * inverse_rms * gain_vec.astype(jnp.float32)).astype(jnp.bfloat16)

def widen(rounded):
    return lax.optimization_barrier(rounded).astype(jnp.float32)

def rotate(vectors, positions):
    half_dim = vectors.shape[-1] // 2
    frequency = 10000.0 ** (-2.0 * jnp.arange(half_dim, dtype=jnp.float32) / (2 * half_dim))
    angles = positions.astype(jnp.float32)[:, None, None] * frequency
    cosines = jnp.cos(angles)
    sines = jnp.sin(angles)
    first_half = vectors[..., :half_dim]
    second = vectors[..., half_dim:]
    return jnp.concatenate([first_half * cosines - second * sines, second * cosines + first_half * sines], axis=-1)

def attend(queries, keys_wide, values_wide, live_slots, new_keys, new_values, query_steps):
    inverse_root = 1.0 / math.sqrt(queries.shape[-1])
    cache_scores = jnp.einsum('rhqd,rhld->rhql', queries, keys_wide) * inverse_root
    cache_scores = jnp.where(live_slots[:, None, None, :], cache_scores, masked)
    new_scores = jnp.einsum('rhqd,rhsd->rhqs', queries, new_keys) * inverse_root
    causal = jnp.arange(new_keys.shape[2], dtype=jnp.int32)[None, :] <= query_steps[:, None]
    new_scores = jnp.where(causal[None, None], new_scores, masked)
    row_max = jnp.maximum(lax.optimization_barrier(jnp.max(cache_scores, axis=-1, keepdims=True)), lax.optimization_barrier(jnp.max(new_scores, axis=-1, keepdims=True)))
    cache_weights = jnp.exp(cache_scores - row_max)
    new_weights = jnp.exp(new_scores - row_max)
    weight_total = lax.optimization_barrier(jnp.sum(cache_weights, axis=-1)) + lax.optimization_barrier(jnp.sum(new_weights, axis=-1))
    mixed = jnp.einsum('rhql,rhld->rhqd', widen(cache_weights.astype(jnp.bfloat16)), values_wide)
    mixed = mixed + jnp.einsum('rhqs,rhsd->rhqd', widen(new_weights.astype(jnp.bfloat16)), new_values)
    return (mixed / weight_total[..., None]).astype(jnp.bfloat16)

def reference(step_ids, prompt_lens, embed_table, attn_gain, w_qkv, w_out, key_cache, value_cache, reward_pieces, piece_lens, reward_gain, w_value, b_value, w_score, b_score):
    row_count = step_ids.shape[0]
    cache_slots = jnp.arange(CACHE_LEN, dtype=jnp.int32)
    live_slots = cache_slots[None, :] < prompt_lens[:, None]
    keys_wide = key_cache.astype(jnp.float32)
    values_wide = value_cache.astype(jnp.float32)
    weights_wide = w_qkv.astype(jnp.float32)
    key_list = []
    value_list = []
    results = []
    for step_index in range(STEPS):
        embedded = jnp.take(embed_table, step_ids[:, step_index], axis=0)
        normed = normalize(embedded, attn_gain)
        projected = jnp.einsum('nd,cde->nce', widen(normed), weights_wide).reshape(row_count, 3, HEADS, HD)
        positions = prompt_lens + step_index
        queries = rotate(projected[:, 0], positions).astype(jnp.bfloat16)
        new_key = rotate(projected[:, 1], positions).astype(jnp.bfloat16)
        new_value = projected[:, 2].astype(jnp.bfloat16)
        key_list.append(widen(new_key)[:, :, None, :])
        value_list.append(widen(new_value)[:, :, None, :])
        head_out = attend(widen(queries)[:, :, None, :], keys_wide, values_wide, live_slots, jnp.concatenate(key_list, axis=2), jnp.concatenate(value_list, axis=2), jnp.array([step_index], dtype=jnp.int32))
        results.append(jnp.dot(head_out.reshape(row_count, -1), w_out, preferred_element_type=jnp.float32).astype(jnp.bfloat16))
    attn_out = jnp.stack(results, axis=1)

    def score_piece(inputs):
        piece_rows, length = inputs
        normed_piece = normalize(piece_rows, reward_gain)
        preact = jnp.dot(normed_piece, w_value, preferred_element_type=jnp.float32) + b_value
        hidden = jax.nn.silu(preact)
        scored = jnp.dot(hidden, w_score, precision=lax.Precision.HIGHEST) + b_score[0]
        positions = jnp.arange(SEQ, dtype=jnp.int32)
        return jnp.where(positions < length, scored, 0.0)
    piece_values = lax.map(score_piece, (reward_pieces, piece_lens))
    return (attn_out, piece_values)
```

```python
import functools
import math

import jax
import jax.numpy as jnp
from jax import lax
from jax.experimental import pallas as pl
from jax.experimental.pallas import tpu as pltpu
from jax.sharding import Mesh, PartitionSpec as P

EPS = 1e-05
MASKED = -1e30
DP = ("yhi", "core")
MP = ("x", "z", "ylo")
GROUP = 32
LANES = 128
TILE = 256
COLS = 512


def vmem():
    return pl.BlockSpec(memory_space=pltpu.VMEM)


def hbm():
    return pl.BlockSpec(memory_space=pl.ANY)


def attention_kernel(emb_ref, gain_ref, wqkv_ref, cos_ref, sin_ref, lens_ref, key_ref, value_ref, out_ref, normed_ref):
    tokens = emb_ref.shape[1]
    width = GROUP * LANES
    rows = key_ref.shape[0]
    steps = tokens // rows
    squares = jnp.zeros((tokens, LANES), jnp.float32)
    for s in range(GROUP):
        part = emb_ref[s].astype(jnp.float32)
        squares = squares + part * part
    mean = jnp.sum(squares, axis=-1, keepdims=True) / width
    inverse_rms = lax.rsqrt(mean + EPS)
    for s in range(GROUP):
        part = emb_ref[s].astype(jnp.float32) * inverse_rms * gain_ref[s : s + 1, :]
        normed_ref[:, s * LANES : (s + 1) * LANES] = part.astype(jnp.bfloat16)
    normed = normed_ref[...]
    parts = [jnp.dot(normed, wqkv_ref[c], preferred_element_type=jnp.float32) for c in range(3)]
    cos, sin = cos_ref[...], sin_ref[...]
    half = LANES // 2

    def rotate(v):
        return (v * cos + pltpu.roll(v, half, 1) * sin).astype(jnp.bfloat16)

    queries, new_keys = rotate(parts[0]), rotate(parts[1])
    new_values = parts[2].astype(jnp.bfloat16)
    root = 1.0 / math.sqrt(LANES)
    slots = key_ref.shape[1]
    group_of = lax.broadcasted_iota(jnp.int32, (tokens, slots), 0) // steps
    scores = jnp.zeros((tokens, slots), jnp.float32)
    for r in range(rows):
        one = lax.dot_general(queries, key_ref[r], (((1,), (1,)), ((), ())), preferred_element_type=jnp.float32)
        scores = jnp.where(group_of == r, one, scores)
    live = lax.broadcasted_iota(jnp.int32, (tokens, slots), 1) < lens_ref[:, 0:1]
    scores = jnp.where(live, scores * root, MASKED)
    fresh = lax.dot_general(queries, new_keys, (((1,), (1,)), ((), ())), preferred_element_type=jnp.float32)
    i = lax.broadcasted_iota(jnp.int32, (tokens, tokens), 0)
    j = lax.broadcasted_iota(jnp.int32, (tokens, tokens), 1)
    causal = (i // steps == j // steps) & (j <= i)
    fresh = jnp.where(causal, fresh * root, MASKED)
    top = jnp.maximum(jnp.max(scores, axis=-1, keepdims=True), jnp.max(fresh, axis=-1, keepdims=True))
    weights = jnp.exp(scores - top)
    fresh_weights = jnp.exp(fresh - top)
    total = jnp.sum(weights, axis=-1, keepdims=True) + jnp.sum(fresh_weights, axis=-1, keepdims=True)
    mixed = jnp.dot(fresh_weights.astype(jnp.bfloat16), new_values, preferred_element_type=jnp.float32)
    for r in range(rows):
        own = jnp.where(group_of == r, weights, 0.0).astype(jnp.bfloat16)
        mixed = mixed + jnp.dot(own, value_ref[r], preferred_element_type=jnp.float32)
    out_ref[...] = (mixed / total).astype(jnp.bfloat16)


def attention(emb, gain, w_qkv, cos, sin, lens, keys, values):
    tokens = emb.shape[1]
    return pl.pallas_call(
        attention_kernel,
        out_shape=jax.ShapeDtypeStruct((tokens, LANES), jnp.bfloat16),
        in_specs=[vmem()] * 8,
        out_specs=vmem(),
        scratch_shapes=[pltpu.VMEM((tokens, GROUP * LANES), jnp.bfloat16)],
        compiler_params=pltpu.CompilerParams(vmem_limit_bytes=24 << 20),
        cost_estimate=pl.CostEstimate(flops=4 * 10**8, bytes_accessed=24 << 20, transcendentals=40000),
        name="attention",
    )(emb, gain, w_qkv, cos, sin, lens, keys, values)


def project_kernel(first, second, rows, w_ref, heads_ref, out_ref, w_buf, heads_buf, flat, sems):
    tokens = heads_buf.shape[1]
    w_copy = pltpu.make_async_copy(w_ref.at[:, pl.ds(first, rows), :], w_buf, sems.at[0])
    heads_copy = pltpu.make_async_copy(heads_ref.at[:, pl.ds(second, tokens), :], heads_buf, sems.at[1])
    w_copy.start()
    heads_copy.start()
    w_copy.wait()
    heads_copy.wait()
    for s in range(GROUP):
        flat[:, s * LANES : (s + 1) * LANES] = heads_buf[s]
    w = w_buf[...].reshape(GROUP * rows, LANES)
    out_ref[...] = jnp.dot(flat[...], w, preferred_element_type=jnp.float32).astype(jnp.bfloat16)


def project(w_message, w_row, heads_message, heads_row, tokens):
    return pl.pallas_call(
        functools.partial(project_kernel, w_row, heads_row, LANES),
        out_shape=jax.ShapeDtypeStruct((tokens, LANES), jnp.bfloat16),
        in_specs=[hbm(), hbm()],
        out_specs=vmem(),
        scratch_shapes=[
            pltpu.VMEM((GROUP, LANES, LANES), jnp.bfloat16),
            pltpu.VMEM((GROUP, tokens, LANES), jnp.bfloat16),
            pltpu.VMEM((tokens, GROUP * LANES), jnp.bfloat16),
            pltpu.SemaphoreType.DMA((2,)),
        ],
        compiler_params=pltpu.CompilerParams(vmem_limit_bytes=16 << 20),
        cost_estimate=pl.CostEstimate(flops=4 * 10**7, bytes_accessed=2 << 20, transcendentals=0),
        name="project",
    )(w_message, heads_message)


def score_kernel(tiles, x_hbm, wa_hbm, wb_hbm, gain_ref, bias_ref, score_ref, out_ref, x_buf, w_buf, normed_ref, x_sems, w_sems):
    width = GROUP * LANES
    span = width // 16

    def x_copy(t):
        return pltpu.make_async_copy(x_hbm.at[:, pl.ds(t * TILE, TILE), :], x_buf.at[t % 2], x_sems.at[t % 2])

    def w_copies(g):
        source = wa_hbm if g < 2 else wb_hbm
        return [
            pltpu.make_async_copy(source.at[k, g % 2], w_buf.at[g, pl.ds(k * span, span), :], w_sems.at[g])
            for k in range(16)
        ]

    x_copy(0).start()
    for g in range(4):
        for copy in w_copies(g):
            copy.start()
    for t in range(tiles):
        if t + 1 < tiles:
            x_copy(t + 1).start()
        x_copy(t).wait()
        squares = jnp.zeros((TILE, LANES), jnp.float32)
        for s in range(GROUP):
            part = x_buf[t % 2, s].astype(jnp.float32)
            squares = squares + part * part
        mean = jnp.sum(squares, axis=-1, keepdims=True) / width
        inverse_rms = lax.rsqrt(mean + EPS)
        for s in range(GROUP):
            part = x_buf[t % 2, s].astype(jnp.float32) * inverse_rms * gain_ref[s : s + 1, :]
            normed_ref[:, s * LANES : (s + 1) * LANES] = part.astype(jnp.bfloat16)
        total = jnp.zeros((TILE, LANES), jnp.float32)
        for g in range(4):
            if t == 0:
                pltpu.make_async_copy(w_buf.at[g], w_buf.at[g], w_sems.at[g]).wait()
            pre = jnp.dot(normed_ref[...], w_buf[g], preferred_element_type=jnp.float32)
            pre = pre + bias_ref[g : g + 1, :]
            hidden = pre / (1.0 + jnp.exp(-pre)) * score_ref[g : g + 1, :]
            for c in range(COLS // LANES):
                total = total + hidden[:, c * LANES : (c + 1) * LANES]
        out_ref[t : t + 1, :] = jnp.sum(total.T, axis=0, keepdims=True)


def score_rows(message, count, w_own, w_other, gain, bias, w_score):
    tiles = count // TILE
    width = GROUP * LANES
    return pl.pallas_call(
        functools.partial(score_kernel, tiles),
        out_shape=jax.ShapeDtypeStruct((tiles, TILE), jnp.float32),
        in_specs=[hbm(), hbm(), hbm(), vmem(), vmem(), vmem()],
        out_specs=vmem(),
        scratch_shapes=[
            pltpu.VMEM((2, GROUP, TILE, LANES), jnp.bfloat16),
            pltpu.VMEM((4, width, COLS), jnp.bfloat16),
            pltpu.VMEM((TILE, width), jnp.bfloat16),
            pltpu.SemaphoreType.DMA((2,)),
            pltpu.SemaphoreType.DMA((4,)),
        ],
        compiler_params=pltpu.CompilerParams(vmem_limit_bytes=40 << 20),
        cost_estimate=pl.CostEstimate(
            flops=2 * count * width * 4 * COLS, bytes_accessed=24 << 20, transcendentals=count * 4 * COLS
        ),
        name="score",
    )(message, w_own, w_other, gain, bias, w_score)


def exchange(message):
    return lax.all_to_all(message, MP, 0, 0)


def spread(block):
    return exchange(jnp.broadcast_to(block[None], (GROUP,) + block.shape))


def per_device(
    step_ids,
    prompt_lens,
    embed_table,
    attn_gain,
    w_qkv,
    w_out,
    key_cache,
    value_cache,
    reward_pieces,
    piece_lens,
    reward_gain,
    w_value,
    b_value,
    w_score,
    b_score,
):
    rows, steps = step_ids.shape
    tokens = rows * steps
    core = lax.axis_index("core")
    yhi = lax.axis_index("yhi")
    me = lax.axis_index(MP)

    quarter = lax.dynamic_slice_in_dim(w_value, (core * 2 + yhi) * COLS, COLS, axis=1)
    w_own = lax.all_gather(quarter[None], ("x", "z", "yhi", "ylo"), axis=0, tiled=True)
    w_own = w_own.reshape(16, 2, 2 * LANES, COLS)
    w_other = lax.ppermute(w_own, "core", [(0, 1), (1, 0)])
    order = jnp.stack([core, 1 - core])
    bias = b_value.reshape(2, 2, COLS)[order].reshape(4, COLS)
    score = w_score.reshape(2, 2, COLS)[order].reshape(4, COLS)

    local = embed_table.at[step_ids.reshape(tokens)].get(mode="promise_in_bounds")
    embedded = spread(local)
    half_dim = LANES // 2
    frequency = 10000.0 ** (-2.0 * jnp.arange(half_dim, dtype=jnp.float32) / (2 * half_dim))
    positions = (prompt_lens[:, None] + jnp.arange(steps, dtype=jnp.int32)[None, :]).reshape(tokens)
    angles = positions.astype(jnp.float32)[:, None] * frequency
    cos = jnp.concatenate([jnp.cos(angles)] * 2, axis=-1)
    sin = jnp.concatenate([-jnp.sin(angles), jnp.sin(angles)], axis=-1)
    lens = jnp.broadcast_to(jnp.repeat(prompt_lens, steps)[:, None], (tokens, LANES))
    heads = attention(
        embedded,
        attn_gain.astype(jnp.float32).reshape(GROUP, LANES),
        w_qkv,
        cos,
        sin,
        lens,
        key_cache.reshape(rows, -1, LANES),
        value_cache.reshape(rows, -1, LANES),
    )

    pieces, length, _ = reward_pieces.shape
    here = length // GROUP
    blocks = reward_pieces.reshape(pieces, GROUP, here, LANES).transpose(1, 0, 2, 3)
    split = pieces // 2
    count = split * here
    w_blocks = w_out.reshape(LANES, GROUP, LANES).transpose(1, 0, 2)
    first = exchange(jnp.concatenate([blocks[:, :split].reshape(GROUP, count, LANES), w_blocks], axis=1))
    second = exchange(
        jnp.concatenate(
            [
                blocks[:, split:].reshape(GROUP, count, LANES),
                jnp.broadcast_to(heads[None], (GROUP, tokens, LANES)),
            ],
            axis=1,
        )
    )
    gain = reward_gain.astype(jnp.float32).reshape(GROUP, LANES)
    scored = [score_rows(m, count, w_own, w_other, gain, bias, score) for m in (first, second)]
    scored = jnp.concatenate([s.reshape(split, here) for s in scored], axis=0) + b_score[0]
    where = me * here + jnp.arange(here, dtype=jnp.int32)
    piece_values = jnp.where(where[None, :] < piece_lens[:, None], scored, 0.0)

    columns = project(first, count, second, count, tokens)
    attn_out = spread(columns).transpose(1, 0, 2).reshape(rows, steps, GROUP * LANES)
    return (attn_out, piece_values)


def solution(mesh):
    fine = Mesh(mesh.devices.reshape(2, 2, 4, 4, 2), DP + MP)
    return jax.shard_map(
        per_device,
        mesh=fine,
        in_specs=(
            P(DP, None),
            P(DP),
            P(None, MP),
            P(),
            P(None, None, MP),
            P(MP, None),
            P(DP, MP, None, None),
            P(DP, MP, None, None),
            P(DP, None, MP),
            P(DP),
            P(),
            P(MP, None),
            P(),
            P(),
            P(),
        ),
        out_specs=(P(DP, None, None), P(DP, MP)),
        check_vma=False,
    )
```

```python
import functools
import math

import jax
import jax.numpy as jnp
from jax import lax
from jax.experimental import pallas as pl
from jax.experimental.pallas import tpu as pltpu
from jax.sharding import Mesh, PartitionSpec as P

EPS = 1e-05
MASKED = -1e30
DP = ("yhi", "core")
MP = ("x", "z", "ylo")
GROUP = 32
LANES = 128
COLS = 512


def vmem():
    return pl.BlockSpec(memory_space=pltpu.VMEM)


def hbm():
    return pl.BlockSpec(memory_space=pl.ANY)


def attention_kernel(emb_ref, gain_ref, wqkv_ref, cos_ref, sin_ref, lens_ref, key_ref, value_ref, out_ref, normed_ref):
    tokens = emb_ref.shape[1]
    width = GROUP * LANES
    rows = key_ref.shape[0]
    steps = tokens // rows
    squares = jnp.zeros((tokens, LANES), jnp.float32)
    for s in range(GROUP):
        part = emb_ref[s].astype(jnp.float32)
        squares = squares + part * part
    mean = jnp.sum(squares, axis=-1, keepdims=True) / width
    inverse_rms = lax.rsqrt(mean + EPS)
    for s in range(GROUP):
        part = emb_ref[s].astype(jnp.float32) * inverse_rms * gain_ref[s : s + 1, :]
        normed_ref[:, s * LANES : (s + 1) * LANES] = part.astype(jnp.bfloat16)
    normed = normed_ref[...]
    parts = [jnp.dot(normed, wqkv_ref[c], preferred_element_type=jnp.float32) for c in range(3)]
    cos, sin = cos_ref[...], sin_ref[...]
    half = LANES // 2

    def rotate(v):
        return (v * cos + pltpu.roll(v, half, 1) * sin).astype(jnp.bfloat16)

    queries, new_keys = rotate(parts[0]), rotate(parts[1])
    new_values = parts[2].astype(jnp.bfloat16)
    root = 1.0 / math.sqrt(LANES)
    slots = key_ref.shape[1]
    group_of = lax.broadcasted_iota(jnp.int32, (tokens, slots), 0) // steps
    scores = jnp.zeros((tokens, slots), jnp.float32)
    for r in range(rows):
        one = lax.dot_general(queries, key_ref[r], (((1,), (1,)), ((), ())), preferred_element_type=jnp.float32)
        scores = jnp.where(group_of == r, one, scores)
    live = lax.broadcasted_iota(jnp.int32, (tokens, slots), 1) < lens_ref[:, 0:1]
    scores = jnp.where(live, scores * root, MASKED)
    fresh = lax.dot_general(queries, new_keys, (((1,), (1,)), ((), ())), preferred_element_type=jnp.float32)
    i = lax.broadcasted_iota(jnp.int32, (tokens, tokens), 0)
    j = lax.broadcasted_iota(jnp.int32, (tokens, tokens), 1)
    causal = (i // steps == j // steps) & (j <= i)
    fresh = jnp.where(causal, fresh * root, MASKED)
    top = jnp.maximum(jnp.max(scores, axis=-1, keepdims=True), jnp.max(fresh, axis=-1, keepdims=True))
    weights = jnp.exp(scores - top)
    fresh_weights = jnp.exp(fresh - top)
    total = jnp.sum(weights, axis=-1, keepdims=True) + jnp.sum(fresh_weights, axis=-1, keepdims=True)
    mixed = jnp.dot(fresh_weights.astype(jnp.bfloat16), new_values, preferred_element_type=jnp.float32)
    for r in range(rows):
        own = jnp.where(group_of == r, weights, 0.0).astype(jnp.bfloat16)
        mixed = mixed + jnp.dot(own, value_ref[r], preferred_element_type=jnp.float32)
    out_ref[...] = (mixed / total).astype(jnp.bfloat16)


def attention(emb, gain, w_qkv, cos, sin, lens, keys, values):
    tokens = emb.shape[1]
    return pl.pallas_call(
        attention_kernel,
        out_shape=jax.ShapeDtypeStruct((tokens, LANES), jnp.bfloat16),
        in_specs=[vmem()] * 8,
        out_specs=vmem(),
        scratch_shapes=[pltpu.VMEM((tokens, GROUP * LANES), jnp.bfloat16)],
        compiler_params=pltpu.CompilerParams(vmem_limit_bytes=24 << 20),
        cost_estimate=pl.CostEstimate(flops=4 * 10**8, bytes_accessed=24 << 20, transcendentals=40000),
        name="attention",
    )(emb, gain, w_qkv, cos, sin, lens, keys, values)


def project_kernel(first, second, rows, w_ref, heads_ref, out_ref, w_buf, heads_buf, flat, sems):
    tokens = heads_buf.shape[1]
    w_copy = pltpu.make_async_copy(w_ref.at[:, pl.ds(first, rows), :], w_buf, sems.at[0])
    heads_copy = pltpu.make_async_copy(heads_ref.at[:, pl.ds(second, tokens), :], heads_buf, sems.at[1])
    w_copy.start()
    heads_copy.start()
    w_copy.wait()
    heads_copy.wait()
    for s in range(GROUP):
        flat[:, s * LANES : (s + 1) * LANES] = heads_buf[s]
    w = w_buf[...].reshape(GROUP * rows, LANES)
    columns = jnp.dot(flat[...], w, preferred_element_type=jnp.float32).astype(jnp.bfloat16)
    out_ref[...] = columns.astype(jnp.float32)


def project(w_message, w_row, heads_message, heads_row, tokens):
    return pl.pallas_call(
        functools.partial(project_kernel, w_row, heads_row, LANES),
        out_shape=jax.ShapeDtypeStruct((tokens, LANES), jnp.float32),
        in_specs=[hbm(), hbm()],
        out_specs=vmem(),
        scratch_shapes=[
            pltpu.VMEM((GROUP, LANES, LANES), jnp.bfloat16),
            pltpu.VMEM((GROUP, tokens, LANES), jnp.bfloat16),
            pltpu.VMEM((tokens, GROUP * LANES), jnp.bfloat16),
            pltpu.SemaphoreType.DMA((2,)),
        ],
        compiler_params=pltpu.CompilerParams(vmem_limit_bytes=16 << 20),
        cost_estimate=pl.CostEstimate(flops=4 * 10**7, bytes_accessed=2 << 20, transcendentals=0),
        name="project",
    )(w_message, heads_message)


def score_kernel(slots, x_hbm, wa_hbm, wb_hbm, gain_ref, bias_ref, score_ref, out_ref, x_buf, w_buf, normed_ref, total_ref, x_sem, w_sems):
    width = GROUP * LANES
    span = width // 16
    rows = slots * LANES
    x_copy = pltpu.make_async_copy(x_hbm.at[:, pl.ds(0, rows), :], x_buf, x_sem.at[0])
    x_copy.start()
    for g in range(4):
        source = wa_hbm if g < 2 else wb_hbm
        for k in range(16):
            pltpu.make_async_copy(source.at[k, g % 2], w_buf.at[g, pl.ds(k * span, span), :], w_sems.at[g]).start()
    x_copy.wait()

    @pl.loop(0, slots)
    def _(q):
        here = pl.ds(pl.multiple_of(q * LANES, LANES), LANES)
        squares = jnp.zeros((LANES, LANES), jnp.float32)
        for s in range(GROUP):
            part = x_buf[s, here, :].astype(jnp.float32)
            squares = squares + part * part
        mean = jnp.sum(squares, axis=-1, keepdims=True) / width
        inverse_rms = lax.rsqrt(mean + EPS)
        for s in range(GROUP):
            part = x_buf[s, here, :].astype(jnp.float32) * inverse_rms * gain_ref[s : s + 1, :]
            normed_ref[here, s * LANES : (s + 1) * LANES] = part.astype(jnp.bfloat16)

    total_ref[...] = jnp.zeros_like(total_ref)

    @pl.loop(0, 4)
    def _(g):
        pltpu.make_async_copy(w_buf.at[g], w_buf.at[g], w_sems.at[g]).wait()
        pre = jnp.dot(normed_ref[...], w_buf[g], preferred_element_type=jnp.float32)
        pre = pre + bias_ref[pl.ds(g, 1), :]
        hidden = pre / (1.0 + jnp.exp(-pre)) * score_ref[pl.ds(g, 1), :]
        total = total_ref[...]
        for c in range(COLS // LANES):
            total = total + hidden[:, c * LANES : (c + 1) * LANES]
        total_ref[...] = total

    for q in range(slots):
        out_ref[q : q + 1, :] = jnp.sum(total_ref[q * LANES : (q + 1) * LANES, :].T, axis=0, keepdims=True)


def score_rows(message, slots, w_own, w_other, gain, bias, w_score):
    width = GROUP * LANES
    rows = slots * LANES
    return pl.pallas_call(
        functools.partial(score_kernel, slots),
        out_shape=jax.ShapeDtypeStruct((slots, LANES), jnp.float32),
        in_specs=[hbm(), hbm(), hbm(), vmem(), vmem(), vmem()],
        out_specs=vmem(),
        scratch_shapes=[
            pltpu.VMEM((GROUP, rows, LANES), jnp.bfloat16),
            pltpu.VMEM((4, width, COLS), jnp.bfloat16),
            pltpu.VMEM((rows, width), jnp.bfloat16),
            pltpu.VMEM((rows, LANES), jnp.float32),
            pltpu.SemaphoreType.DMA((1,)),
            pltpu.SemaphoreType.DMA((4,)),
        ],
        compiler_params=pltpu.CompilerParams(vmem_limit_bytes=56 << 20),
        cost_estimate=pl.CostEstimate(
            flops=2 * rows * width * 4 * COLS, bytes_accessed=24 << 20, transcendentals=rows * 4 * COLS
        ),
        name="score",
    )(message, w_own, w_other, gain, bias, w_score)


def block_starts(lens_ref, pieces):
    starts, counts = [], []
    start = 0
    for i in range(pieces):
        count = lax.shift_right_logical(lens_ref[i] + (LANES - 1), 7)
        starts.append(start)
        counts.append(count)
        start = start + count
    return starts, counts


def pack_kernel(pieces, first, slots, by_column, lens_ref, pieces_ref, extra_ref, out_ref, stage, in_sems, out_sem):
    starts, _ = block_starts(lens_ref, pieces)
    blocks = pieces_ref.shape[1] // LANES
    rows = slots * LANES
    extra = stage.shape[1] - rows
    chunk = GROUP // 4
    for c in range(4):

        @pl.loop(c * chunk, (c + 1) * chunk)
        def _(d):
            for q in range(slots):
                slot = (first + q) * GROUP + d
                piece, start = 0, 0
                for i in range(1, pieces):
                    after = slot >= starts[i]
                    piece = jnp.where(after, i, piece)
                    start = jnp.where(after, starts[i], start)
                block = jnp.minimum(slot - start, blocks - 1)
                pltpu.make_async_copy(
                    pieces_ref.at[piece, pl.ds(pl.multiple_of(block * LANES, LANES), LANES), :],
                    stage.at[d, pl.ds(q * LANES, LANES), :],
                    in_sems.at[c],
                ).start()
            if by_column:
                source = extra_ref.at[:, pl.ds(pl.multiple_of(d * LANES, LANES), LANES)]
            else:
                source = extra_ref
            pltpu.make_async_copy(source, stage.at[d, pl.ds(rows, extra), :], in_sems.at[c]).start()

    for c in range(4):
        part = pl.ds(c * chunk, chunk)
        pltpu.make_async_copy(out_ref.at[part], stage.at[part], in_sems.at[c]).wait()
        pltpu.make_async_copy(stage.at[part], out_ref.at[part], out_sem.at[c]).start()
    for c in range(4):
        part = pl.ds(c * chunk, chunk)
        pltpu.make_async_copy(stage.at[part], out_ref.at[part], out_sem.at[c]).wait()


def pack(piece_lens, pieces, extra, first, slots, by_column):
    rows = slots * LANES + extra.shape[0]
    return pl.pallas_call(
        functools.partial(pack_kernel, pieces.shape[0], first, slots, by_column),
        out_shape=jax.ShapeDtypeStruct((GROUP, rows, LANES), jnp.bfloat16),
        in_specs=[pl.BlockSpec(memory_space=pltpu.SMEM), hbm(), hbm()],
        out_specs=pl.BlockSpec(memory_space=pltpu.HBM),
        scratch_shapes=[
            pltpu.VMEM((GROUP, rows, LANES), jnp.bfloat16),
            pltpu.SemaphoreType.DMA((4,)),
            pltpu.SemaphoreType.DMA((4,)),
        ],
        compiler_params=pltpu.CompilerParams(vmem_limit_bytes=24 << 20),
        cost_estimate=pl.CostEstimate(flops=0, bytes_accessed=4 * GROUP * rows * LANES, transcendentals=0),
        name="pack",
    )(piece_lens, pieces, extra)


def finish_kernel(pieces, tokens, scalars_ref, offset_ref, result_ref, attn_ref, value_ref):
    starts, counts = block_starts(scalars_ref, pieces)
    me = scalars_ref[pieces]
    where = me * LANES + lax.broadcasted_iota(jnp.int32, (1, LANES), 1)
    for i in range(pieces):
        slot = jnp.minimum(starts[i] + jnp.minimum(me, counts[i]), pieces * GROUP - 1)
        row = result_ref[slot & (GROUP - 1), pl.ds(tokens + lax.shift_right_logical(slot, 5), 1), :]
        value_ref[i : i + 1, :] = jnp.where(where < scalars_ref[i], row + offset_ref[0], 0.0)
    for s in range(GROUP):
        attn_ref[:, s * LANES : (s + 1) * LANES] = result_ref[s, 0:tokens, :].astype(jnp.bfloat16)


def finish(scalars, offset, result, pieces, tokens):
    return pl.pallas_call(
        functools.partial(finish_kernel, pieces, tokens),
        out_shape=(
            jax.ShapeDtypeStruct((tokens, GROUP * LANES), jnp.bfloat16),
            jax.ShapeDtypeStruct((pieces, LANES), jnp.float32),
        ),
        in_specs=[pl.BlockSpec(memory_space=pltpu.SMEM)] * 2 + [vmem()],
        out_specs=(vmem(), vmem()),
        compiler_params=pltpu.CompilerParams(vmem_limit_bytes=16 << 20),
        name="finish",
    )(scalars, offset, result)


def exchange(message):
    return lax.all_to_all(message, MP, 0, 0)


def spread(block):
    return exchange(jnp.broadcast_to(block[None], (GROUP,) + block.shape))


def per_device(
    step_ids,
    prompt_lens,
    embed_table,
    attn_gain,
    w_qkv,
    w_out,
    key_cache,
    value_cache,
    reward_pieces,
    piece_lens,
    reward_gain,
    w_value,
    b_value,
    w_score,
    b_score,
):
    rows, steps = step_ids.shape
    tokens = rows * steps
    core = lax.axis_index("core")
    yhi = lax.axis_index("yhi")
    me = lax.axis_index(MP)

    quarter = lax.dynamic_slice_in_dim(w_value, (core * 2 + yhi) * COLS, COLS, axis=1)
    w_own = lax.all_gather(quarter[None], ("x", "z", "yhi", "ylo"), axis=0, tiled=True)
    w_own = w_own.reshape(16, 2, 2 * LANES, COLS)
    order = jnp.stack([core, 1 - core])
    bias = b_value.reshape(2, 2, COLS)[order].reshape(4, COLS)
    score = w_score.reshape(2, 2, COLS)[order].reshape(4, COLS)

    local = embed_table.at[step_ids.reshape(tokens)].get(mode="promise_in_bounds")
    embedded = spread(local)
    half_dim = LANES // 2
    frequency = 10000.0 ** (-2.0 * jnp.arange(half_dim, dtype=jnp.float32) / (2 * half_dim))
    positions = (prompt_lens[:, None] + jnp.arange(steps, dtype=jnp.int32)[None, :]).reshape(tokens)
    angles = positions.astype(jnp.float32)[:, None] * frequency
    cos = jnp.concatenate([jnp.cos(angles)] * 2, axis=-1)
    sin = jnp.concatenate([-jnp.sin(angles), jnp.sin(angles)], axis=-1)
    lens = jnp.broadcast_to(jnp.repeat(prompt_lens, steps)[:, None], (tokens, LANES))
    attend = lambda embedded: attention(
        embedded,
        attn_gain.astype(jnp.float32).reshape(GROUP, LANES),
        w_qkv,
        cos,
        sin,
        lens,
        key_cache.reshape(rows, -1, LANES),
        value_cache.reshape(rows, -1, LANES),
    )

    pieces, length, _ = reward_pieces.shape
    total = jnp.sum((piece_lens + (LANES - 1)) // LANES)
    most = jnp.full((8, LANES), total, jnp.int32).astype(jnp.float32)
    for axis in ("core", "yhi"):
        most = jnp.maximum(most, lax.ppermute(most, axis, [(0, 1), (1, 0)]))
    base = length // LANES * pieces // GROUP // 2
    rest = jnp.clip((most[0, 0].astype(jnp.int32) + (GROUP - 1)) // GROUP - base, 0, base)

    message = pack(piece_lens, reward_pieces, w_out, 0, base, True)
    message, embedded = lax.optimization_barrier((message, embedded))
    first = exchange(message)
    heads = attend(embedded)
    gain = reward_gain.astype(jnp.float32).reshape(GROUP, LANES)

    def remainder(slots, first, heads, w_own, piece_lens, reward_pieces, gain, bias, score):
        w_other = lax.ppermute(w_own, "core", [(0, 1), (1, 0)])
        second = exchange(pack(piece_lens, reward_pieces, heads, base, slots, False))
        parts = [score_rows(first, base, w_own, w_other, gain, bias, score)]
        if slots:
            parts.append(score_rows(second, slots, w_own, w_other, gain, bias, score))
        if slots < base:
            parts.append(jnp.zeros((base - slots, LANES), jnp.float32))
        columns = project(first, base * LANES, second, slots * LANES, tokens)
        return jnp.concatenate([columns] + parts, axis=0)

    payload = lax.switch(
        rest,
        [functools.partial(remainder, slots) for slots in range(base + 1)],
        first,
        heads,
        w_own,
        piece_lens,
        reward_pieces,
        gain,
        bias,
        score,
    )
    scalars = jnp.concatenate([piece_lens, me.reshape(1).astype(jnp.int32)])
    attn_out, piece_values = finish(scalars, b_score, spread(payload), pieces, tokens)
    return (attn_out.reshape(rows, steps, GROUP * LANES), piece_values)


def solution(mesh):
    fine = Mesh(mesh.devices.reshape(2, 2, 4, 4, 2), DP + MP)
    return jax.shard_map(
        per_device,
        mesh=fine,
        in_specs=(
            P(DP, None),
            P(DP),
            P(None, MP),
            P(),
            P(None, None, MP),
            P(MP, None),
            P(DP, MP, None, None),
            P(DP, MP, None, None),
            P(DP, None, MP),
            P(DP),
            P(),
            P(MP, None),
            P(),
            P(),
            P(),
        ),
        out_specs=(P(DP, None, None), P(DP, MP)),
        check_vma=False,
    )
```

```python
import functools
import math

import jax
import jax.numpy as jnp
from jax import lax
from jax.experimental import pallas as pl
from jax.experimental.pallas import tpu as pltpu
from jax.sharding import Mesh, PartitionSpec as P

EPS = 1e-05
MASKED = -1e30
DP = ("yhi", "core")
MP = ("x", "z", "ylo")
GROUP = 32
LANES = 128
COLS = 512
SPAN = 256
HALF = 256
CHUNK = 4
NEAR = (0, -1, 1, 2)
RECEIVED = ((0, (0, 1, 2, 3)), (-1, (0, 1, 2, 3)), (1, (0, 1, 2, 3)), (2, (0, 1)), (2, (2, 3)))


def vmem():
    return pl.BlockSpec(memory_space=pltpu.VMEM)


def hbm():
    return pl.BlockSpec(memory_space=pl.ANY)


def lookup_kernel(ids_ref, table_ref, out_ref, tiles, picked, sem):
    rows, steps = ids_ref.shape
    for i in range(rows * steps):
        first = lax.shift_right_logical(ids_ref[i // steps, i % steps], 3) * 8
        pltpu.make_async_copy(table_ref.at[pl.ds(pl.multiple_of(first, 8), 8), :], tiles.at[i], sem.at[0]).start()
    pltpu.make_async_copy(tiles, tiles, sem.at[0]).wait()
    sublane = lax.broadcasted_iota(jnp.int32, (8, LANES), 0)
    for i in range(rows * steps):
        own = sublane == (ids_ref[i // steps, i % steps] & 7)
        picked[i : i + 1, :] = jnp.sum(jnp.where(own, tiles[i].astype(jnp.float32), 0.0), axis=0, keepdims=True)
    block = picked[...].astype(jnp.bfloat16)
    for d in range(GROUP):
        out_ref[d] = block


def lookup(step_ids, embed_table):
    tokens = step_ids.shape[0] * step_ids.shape[1]
    return pl.pallas_call(
        lookup_kernel,
        out_shape=jax.ShapeDtypeStruct((GROUP, tokens, LANES), jnp.bfloat16),
        in_specs=[pl.BlockSpec(memory_space=pltpu.SMEM), pl.BlockSpec(memory_space=pltpu.HBM)],
        out_specs=vmem(),
        scratch_shapes=[
            pltpu.VMEM((tokens, 8, LANES), jnp.bfloat16),
            pltpu.VMEM((tokens, LANES), jnp.float32),
            pltpu.SemaphoreType.DMA((1,)),
        ],
        compiler_params=pltpu.CompilerParams(vmem_limit_bytes=60 << 20),
        name="lookup",
    )(step_ids, embed_table)


def attention_kernel(emb_ref, gain_ref, wqkv_ref, cos_ref, sin_ref, lens_ref, key_ref, value_ref, wout_ref, out_ref, normed_ref):
    tokens = emb_ref.shape[1]
    width = GROUP * LANES
    rows = key_ref.shape[0]
    steps = tokens // rows
    squares = jnp.zeros((tokens, LANES), jnp.float32)
    for s in range(GROUP):
        part = emb_ref[s].astype(jnp.float32)
        squares = squares + part * part
    mean = jnp.sum(squares, axis=-1, keepdims=True) / width
    inverse_rms = lax.rsqrt(mean + EPS)
    for s in range(GROUP):
        part = emb_ref[s].astype(jnp.float32) * inverse_rms * gain_ref[s : s + 1, :]
        normed_ref[:, s * LANES : (s + 1) * LANES] = part.astype(jnp.bfloat16)
    normed = normed_ref[...]
    parts = [jnp.dot(normed, wqkv_ref[c], preferred_element_type=jnp.float32) for c in range(3)]
    cos, sin = cos_ref[...], sin_ref[...]
    half = LANES // 2

    def rotate(v):
        return (v * cos + pltpu.roll(v, half, 1) * sin).astype(jnp.bfloat16)

    queries, new_keys = rotate(parts[0]), rotate(parts[1])
    new_values = parts[2].astype(jnp.bfloat16)
    root = 1.0 / math.sqrt(LANES)
    slots = key_ref.shape[1]
    group_of = lax.broadcasted_iota(jnp.int32, (tokens, slots), 0) // steps
    scores = jnp.zeros((tokens, slots), jnp.float32)
    for r in range(rows):
        one = lax.dot_general(queries, key_ref[r], (((1,), (1,)), ((), ())), preferred_element_type=jnp.float32)
        scores = jnp.where(group_of == r, one, scores)
    live = lax.broadcasted_iota(jnp.int32, (tokens, slots), 1) < lens_ref[:, 0:1]
    scores = jnp.where(live, scores * root, MASKED)
    fresh = lax.dot_general(queries, new_keys, (((1,), (1,)), ((), ())), preferred_element_type=jnp.float32)
    i = lax.broadcasted_iota(jnp.int32, (tokens, tokens), 0)
    j = lax.broadcasted_iota(jnp.int32, (tokens, tokens), 1)
    causal = (i // steps == j // steps) & (j <= i)
    fresh = jnp.where(causal, fresh * root, MASKED)
    top = jnp.maximum(jnp.max(scores, axis=-1, keepdims=True), jnp.max(fresh, axis=-1, keepdims=True))
    weights = jnp.exp(scores - top)
    fresh_weights = jnp.exp(fresh - top)
    total = jnp.sum(weights, axis=-1, keepdims=True) + jnp.sum(fresh_weights, axis=-1, keepdims=True)
    mixed = jnp.dot(fresh_weights.astype(jnp.bfloat16), new_values, preferred_element_type=jnp.float32)
    for r in range(rows):
        own = jnp.where(group_of == r, weights, 0.0).astype(jnp.bfloat16)
        mixed = mixed + jnp.dot(own, value_ref[r], preferred_element_type=jnp.float32)
    heads = (mixed / total).astype(jnp.bfloat16)
    partial = jnp.dot(heads, wout_ref[...], preferred_element_type=jnp.float32)
    high = partial.astype(jnp.bfloat16)
    out_ref[0:tokens, :] = high
    out_ref[tokens:, :] = (partial - high.astype(jnp.float32)).astype(jnp.bfloat16)


def attention(emb, gain, w_qkv, cos, sin, lens, keys, values, w_out):
    tokens = emb.shape[1]
    return pl.pallas_call(
        attention_kernel,
        out_shape=jax.ShapeDtypeStruct((2 * tokens, GROUP * LANES), jnp.bfloat16),
        in_specs=[vmem()] * 9,
        out_specs=vmem(),
        scratch_shapes=[pltpu.VMEM((tokens, GROUP * LANES), jnp.bfloat16)],
        compiler_params=pltpu.CompilerParams(vmem_limit_bytes=24 << 20),
        cost_estimate=pl.CostEstimate(flops=4 * 10**8, bytes_accessed=24 << 20, transcendentals=40000),
        name="attention",
    )(emb, gain, w_qkv, cos, sin, lens, keys, values, w_out)


def combine_kernel(first, message_ref, out_ref, buf, sem):
    tokens = out_ref.shape[0]
    copy = pltpu.make_async_copy(message_ref.at[:, pl.ds(first, 2 * tokens), :], buf, sem.at[0])
    copy.start()
    copy.wait()
    total = jnp.zeros((tokens, LANES), jnp.float32)
    for s in range(GROUP):
        total = total + (buf[s, 0:tokens, :].astype(jnp.float32) + buf[s, tokens:, :].astype(jnp.float32))
    out_ref[...] = total.astype(jnp.bfloat16).astype(jnp.float32)


def combine(message, first, tokens):
    return pl.pallas_call(
        functools.partial(combine_kernel, first),
        out_shape=jax.ShapeDtypeStruct((tokens, LANES), jnp.float32),
        in_specs=[hbm()],
        out_specs=vmem(),
        scratch_shapes=[pltpu.VMEM((GROUP, 2 * tokens, LANES), jnp.bfloat16), pltpu.SemaphoreType.DMA((1,))],
        compiler_params=pltpu.CompilerParams(vmem_limit_bytes=60 << 20),
        cost_estimate=pl.CostEstimate(flops=10**5, bytes_accessed=1 << 19, transcendentals=0),
        name="combine",
    )(message)


def score_kernel(slots, place_ref, x_hbm, *refs):
    w_hbm, (gain_ref, bias_ref, score_ref, out_ref) = refs[:10], refs[10:14]
    x_buf, w_buf, normed_ref, total_ref, x_sem, w_sems = refs[14:]
    width = GROUP * LANES
    rows = slots * LANES
    x_copy = pltpu.make_async_copy(x_hbm.at[:, pl.ds(0, rows), :], x_buf, x_sem.at[0])
    x_copy.start()
    core, x, z = place_ref[0], place_ref[1], place_ref[2]
    for side in range(2):
        for h in range(2):
            owner = core if side == 0 else 1 - core
            near = jnp.where(owner == 0, z, x)
            far = jnp.where(owner == 0, x, z)
            for index, (step, firsts) in enumerate(RECEIVED):
                last = (far + step) & 3
                for row, a in enumerate(firsts):
                    mine = (near + NEAR[a]) & 3
                    block = jnp.where(owner == 0, last * 4 + mine, mine * 4 + last)
                    g = owner * 2 + h
                    pltpu.make_async_copy(
                        w_hbm[side * 5 + index].at[pl.ds(row * SPAN, SPAN), pl.ds(h * COLS, COLS)],
                        w_buf.at[g, pl.ds(pl.multiple_of(block * SPAN, SPAN), SPAN), :],
                        w_sems.at[g],
                    ).start()
    x_copy.wait()

    @pl.loop(0, slots)
    def _(q):
        here = pl.ds(pl.multiple_of(q * LANES, LANES), LANES)

        def square(c, squares):
            for i in range(CHUNK):
                part = x_buf[c * CHUNK + i, here, :].astype(jnp.float32)
                squares = squares + part * part
            return squares

        squares = lax.fori_loop(0, GROUP // CHUNK, square, jnp.zeros((LANES, LANES), jnp.float32))
        mean = jnp.sum(squares, axis=-1, keepdims=True) / width
        inverse_rms = lax.rsqrt(mean + EPS)

        @pl.loop(0, GROUP // CHUNK)
        def _(c):
            for i in range(CHUNK):
                s = c * CHUNK + i
                part = x_buf[s, here, :].astype(jnp.float32) * inverse_rms * gain_ref[pl.ds(s, 1), :]
                normed_ref[here, pl.ds(pl.multiple_of(s * LANES, LANES), LANES)] = part.astype(jnp.bfloat16)

    total_ref[...] = jnp.zeros_like(total_ref)

    @pl.loop(0, 4)
    def _(i):
        g = jnp.where(i < 2, core, 1 - core) * 2 + (i & 1)
        pltpu.make_async_copy(w_buf.at[g], w_buf.at[g], w_sems.at[g]).wait()
        bias, score = bias_ref[pl.ds(g, 1), :], score_ref[pl.ds(g, 1), :]
        for part in range(0, rows, HALF):
            some = slice(part, min(part + HALF, rows))
            pre = jnp.dot(normed_ref[some, :], w_buf[g], preferred_element_type=jnp.float32) + bias
            hidden = pre / (1.0 + jnp.exp(-pre)) * score
            total = total_ref[some, :]
            for c in range(COLS // LANES):
                total = total + hidden[:, c * LANES : (c + 1) * LANES]
            total_ref[some, :] = total

    for q in range(slots):
        out_ref[q : q + 1, :] = jnp.sum(total_ref[q * LANES : (q + 1) * LANES, :].T, axis=0, keepdims=True)


def score_rows(message, slots, place, parts, gain, bias, w_score):
    width = GROUP * LANES
    rows = slots * LANES
    return pl.pallas_call(
        functools.partial(score_kernel, slots),
        out_shape=jax.ShapeDtypeStruct((slots, LANES), jnp.float32),
        in_specs=[pl.BlockSpec(memory_space=pltpu.SMEM)] + [hbm()] * 11 + [vmem()] * 3,
        out_specs=vmem(),
        scratch_shapes=[
            pltpu.VMEM((GROUP, rows, LANES), jnp.bfloat16),
            pltpu.VMEM((4, width, COLS), jnp.bfloat16),
            pltpu.VMEM((rows, width), jnp.bfloat16),
            pltpu.VMEM((rows, LANES), jnp.float32),
            pltpu.SemaphoreType.DMA((1,)),
            pltpu.SemaphoreType.DMA((4,)),
        ],
        compiler_params=pltpu.CompilerParams(vmem_limit_bytes=60 << 20),
        cost_estimate=pl.CostEstimate(
            flops=2 * rows * width * 4 * COLS, bytes_accessed=24 << 20, transcendentals=rows * 4 * COLS
        ),
        name="score",
    )(place, message, *parts, gain, bias, w_score)


def block_starts(lens_ref, pieces):
    starts, counts = [], []
    start = 0
    for i in range(pieces):
        count = lax.shift_right_logical(lens_ref[i] + (LANES - 1), 7)
        starts.append(start)
        counts.append(count)
        start = start + count
    return starts, counts


def pack_kernel(pieces, first, slots, lens_ref, pieces_ref, *refs):
    extra_ref = refs[0] if len(refs) == 5 else None
    out_ref, stage, in_sems, out_sem = refs[-4:]
    starts, _ = block_starts(lens_ref, pieces)
    blocks = pieces_ref.shape[1] // LANES
    rows = slots * LANES
    extra = stage.shape[1] - rows
    chunk = GROUP // 4
    for c in range(4):

        @pl.loop(c * chunk, (c + 1) * chunk)
        def _(d):
            for q in range(slots):
                slot = (first + q) * GROUP + d
                piece, start = 0, 0
                for i in range(1, pieces):
                    after = slot >= starts[i]
                    piece = jnp.where(after, i, piece)
                    start = jnp.where(after, starts[i], start)
                block = jnp.minimum(slot - start, blocks - 1)
                pltpu.make_async_copy(
                    pieces_ref.at[piece, pl.ds(pl.multiple_of(block * LANES, LANES), LANES), :],
                    stage.at[d, pl.ds(q * LANES, LANES), :],
                    in_sems.at[c],
                ).start()
            if extra_ref is not None:
                source = extra_ref.at[:, pl.ds(pl.multiple_of(d * LANES, LANES), LANES)]
                pltpu.make_async_copy(source, stage.at[d, pl.ds(rows, extra), :], in_sems.at[c]).start()

    for c in range(4):
        part = pl.ds(c * chunk, chunk)
        pltpu.make_async_copy(out_ref.at[part], stage.at[part], in_sems.at[c]).wait()
        pltpu.make_async_copy(stage.at[part], out_ref.at[part], out_sem.at[c]).start()
    for c in range(4):
        part = pl.ds(c * chunk, chunk)
        pltpu.make_async_copy(stage.at[part], out_ref.at[part], out_sem.at[c]).wait()


def pack(piece_lens, pieces, first, slots, *extra):
    rows = slots * LANES + sum(e.shape[0] for e in extra)
    return pl.pallas_call(
        functools.partial(pack_kernel, pieces.shape[0], first, slots),
        out_shape=jax.ShapeDtypeStruct((GROUP, rows, LANES), jnp.bfloat16),
        in_specs=[pl.BlockSpec(memory_space=pltpu.SMEM), hbm()] + [hbm()] * len(extra),
        out_specs=pl.BlockSpec(memory_space=pltpu.HBM),
        scratch_shapes=[
            pltpu.VMEM((GROUP, rows, LANES), jnp.bfloat16),
            pltpu.SemaphoreType.DMA((4,)),
            pltpu.SemaphoreType.DMA((4,)),
        ],
        compiler_params=pltpu.CompilerParams(vmem_limit_bytes=60 << 20),
        cost_estimate=pl.CostEstimate(flops=0, bytes_accessed=4 * GROUP * rows * LANES, transcendentals=0),
        name="pack",
    )(piece_lens, pieces, *extra)


def finish_kernel(pieces, tokens, scalars_ref, offset_ref, result_ref, attn_ref, value_ref):
    starts, counts = block_starts(scalars_ref, pieces)
    me = scalars_ref[pieces]
    where = me * LANES + lax.broadcasted_iota(jnp.int32, (1, LANES), 1)
    for i in range(pieces):
        slot = jnp.minimum(starts[i] + jnp.minimum(me, counts[i]), pieces * GROUP - 1)
        row = result_ref[slot & (GROUP - 1), pl.ds(tokens + lax.shift_right_logical(slot, 5), 1), :]
        value_ref[i : i + 1, :] = jnp.where(where < scalars_ref[i], row + offset_ref[0], 0.0)
    for s in range(GROUP):
        attn_ref[:, s * LANES : (s + 1) * LANES] = result_ref[s, 0:tokens, :].astype(jnp.bfloat16)


def finish(scalars, offset, result, pieces, tokens):
    return pl.pallas_call(
        functools.partial(finish_kernel, pieces, tokens),
        out_shape=(
            jax.ShapeDtypeStruct((tokens, GROUP * LANES), jnp.bfloat16),
            jax.ShapeDtypeStruct((pieces, LANES), jnp.float32),
        ),
        in_specs=[pl.BlockSpec(memory_space=pltpu.SMEM)] * 2 + [vmem()],
        out_specs=(vmem(), vmem()),
        compiler_params=pltpu.CompilerParams(vmem_limit_bytes=16 << 20),
        name="finish",
    )(scalars, offset, result)


def exchange(message):
    return lax.all_to_all(message, MP, 0, 0)


def spread(block):
    return exchange(jnp.broadcast_to(block[None], (GROUP,) + block.shape))


def shift(value, stage, step):
    pairs = []
    for core in range(2):
        for x in range(4):
            for z in range(4):
                along_x = core != stage
                to = ((x + step) % 4 if along_x else x) * 4 + (z if along_x else (z + step) % 4)
                pairs.append((core * 16 + x * 4 + z, core * 16 + to))
    return lax.ppermute(value, ("core", "x", "z"), pairs)


def around(value, stage):
    half = value.shape[0] // 2
    right, left = shift(value, stage, 1), shift(value, stage, -1)
    return (value, right, left, shift(right[:half], stage, 1), shift(left[half:], stage, -1))


def gather_layer(w_value):
    columns = w_value.shape[1] // 2
    own = lax.dynamic_slice_in_dim(w_value, lax.axis_index("core") * columns, columns, axis=1)
    other = lax.ppermute(own, "ylo", [(0, 1), (1, 0)])
    even = lax.axis_index("ylo") == 0
    pair = jnp.concatenate([jnp.where(even, own, other), jnp.where(even, other, own)], axis=0)
    mine = around(jnp.concatenate(around(pair, 0), axis=0), 1)
    return mine + tuple(lax.ppermute(part, "core", [(0, 1), (1, 0)]) for part in mine)


def per_device(
    step_ids,
    prompt_lens,
    embed_table,
    attn_gain,
    w_qkv,
    w_out,
    key_cache,
    value_cache,
    reward_pieces,
    piece_lens,
    reward_gain,
    w_value,
    b_value,
    w_score,
    b_score,
):
    rows, steps = step_ids.shape
    tokens = rows * steps
    me = lax.axis_index(MP)
    place = jnp.stack([lax.axis_index(name) for name in ("core", "x", "z")]).astype(jnp.int32)
    parts = gather_layer(w_value)
    bias = b_value.reshape(4, COLS)
    score = w_score.reshape(4, COLS)

    embedded = exchange(lookup(step_ids, embed_table))
    half_dim = LANES // 2
    frequency = 10000.0 ** (-2.0 * jnp.arange(half_dim, dtype=jnp.float32) / (2 * half_dim))
    positions = (prompt_lens[:, None] + jnp.arange(steps, dtype=jnp.int32)[None, :]).reshape(tokens)
    angles = positions.astype(jnp.float32)[:, None] * frequency
    cos = jnp.concatenate([jnp.cos(angles)] * 2, axis=-1)
    sin = jnp.concatenate([-jnp.sin(angles), jnp.sin(angles)], axis=-1)
    lens = jnp.broadcast_to(jnp.repeat(prompt_lens, steps)[:, None], (tokens, LANES))
    attend = lambda embedded: attention(
        embedded,
        attn_gain.astype(jnp.float32).reshape(GROUP, LANES),
        w_qkv,
        cos,
        sin,
        lens,
        key_cache.reshape(rows, -1, LANES),
        value_cache.reshape(rows, -1, LANES),
        w_out,
    )

    pieces, length, _ = reward_pieces.shape
    total = jnp.sum((piece_lens + (LANES - 1)) // LANES)
    most = jnp.full((8, LANES), total, jnp.int32).astype(jnp.float32)
    for axis in ("core", "yhi"):
        most = jnp.maximum(most, lax.ppermute(most, axis, [(0, 1), (1, 0)]))
    base = length // LANES * pieces // GROUP // 2
    message = pack(piece_lens, reward_pieces, 0, base)
    message, embedded, most = lax.optimization_barrier((message, embedded, most))
    rest = jnp.clip((most[0, 0].astype(jnp.int32) + (GROUP - 1)) // GROUP - base, 0, base)
    first = exchange(message)
    partial = attend(embedded)
    gain = reward_gain.astype(jnp.float32).reshape(GROUP, LANES)

    def remainder(slots, first, partial, place, piece_lens, reward_pieces, gain, bias, score, *parts):
        second = exchange(pack(piece_lens, reward_pieces, base, slots, partial))
        scored = [score_rows(first, base, place, parts, gain, bias, score)]
        if slots:
            scored.append(score_rows(second, slots, place, parts, gain, bias, score))
        if slots < base:
            scored.append(jnp.zeros((base - slots, LANES), jnp.float32))
        return jnp.concatenate([combine(second, slots * LANES, tokens)] + scored, axis=0)

    payload = lax.switch(
        rest,
        [functools.partial(remainder, slots) for slots in range(base + 1)],
        first,
        partial,
        place,
        piece_lens,
        reward_pieces,
        gain,
        bias,
        score,
        *parts,
    )
    scalars = jnp.concatenate([piece_lens, me.reshape(1).astype(jnp.int32)])
    attn_out, piece_values = finish(scalars, b_score, spread(payload), pieces, tokens)
    return (attn_out.reshape(rows, steps, GROUP * LANES), piece_values)


def solution(mesh):
    fine = Mesh(mesh.devices.reshape(2, 2, 4, 4, 2), DP + MP)
    return jax.shard_map(
        per_device,
        mesh=fine,
        in_specs=(
            P(DP, None),
            P(DP),
            P(None, MP),
            P(),
            P(None, None, MP),
            P(MP, None),
            P(DP, MP, None, None),
            P(DP, MP, None, None),
            P(DP, None, MP),
            P(DP),
            P(),
            P(MP, None),
            P(),
            P(),
            P(),
        ),
        out_specs=(P(DP, None, None), P(DP, MP)),
        check_vma=False,
    )
```

```python
import functools
import math

import jax
import jax.numpy as jnp
from jax import lax
from jax.experimental import pallas as pl
from jax.experimental.pallas import tpu as pltpu
from jax.sharding import Mesh, PartitionSpec as P

EPS = 1e-05
MASKED = -1e30
DP = ("yhi", "core")
MP = ("x", "z", "ylo")
GROUP = 32
LANES = 128
COLS = 512
SPAN = 256
HALF = 256
CHUNK = 4
NEAR = (0, -1, 1, 2)
RECEIVED = ((0, (0, 1, 2, 3)), (-1, (0, 1, 2, 3)), (1, (0, 1, 2, 3)), (2, (0, 1)), (2, (2, 3)))


def vmem():
    return pl.BlockSpec(memory_space=pltpu.VMEM)


def hbm():
    return pl.BlockSpec(memory_space=pl.ANY)


def attention_kernel(row, message_ref, gain_ref, wqkv_hbm, cos_ref, sin_ref, lens_ref, key_hbm, value_hbm, wout_hbm, out_ref, *scratch):
    emb_ref, wqkv_ref, key_ref, value_ref, wout_ref, normed_ref, sems = scratch
    tokens = emb_ref.shape[1]
    copies = [
        pltpu.make_async_copy(source, target, sems.at[i])
        for i, (source, target) in enumerate(
            [
                (message_ref.at[:, pl.ds(row, tokens), :], emb_ref),
                (wqkv_hbm, wqkv_ref),
                (key_hbm, key_ref),
                (value_hbm, value_ref),
                (wout_hbm, wout_ref),
            ]
        )
    ]
    for copy in copies:
        copy.start()
    width = GROUP * LANES
    rows = key_ref.shape[0]
    steps = tokens // rows
    copies[0].wait()
    squares = jnp.zeros((tokens, LANES), jnp.float32)
    for s in range(GROUP):
        part = emb_ref[s].astype(jnp.float32)
        squares = squares + part * part
    mean = jnp.sum(squares, axis=-1, keepdims=True) / width
    inverse_rms = lax.rsqrt(mean + EPS)
    for s in range(GROUP):
        part = emb_ref[s].astype(jnp.float32) * inverse_rms * gain_ref[s : s + 1, :]
        normed_ref[:, s * LANES : (s + 1) * LANES] = part.astype(jnp.bfloat16)
    normed = normed_ref[...]
    copies[1].wait()
    parts = [jnp.dot(normed, wqkv_ref[c], preferred_element_type=jnp.float32) for c in range(3)]
    cos, sin = cos_ref[...], sin_ref[...]
    half = LANES // 2

    def rotate(v):
        return (v * cos + pltpu.roll(v, half, 1) * sin).astype(jnp.bfloat16)

    queries, new_keys = rotate(parts[0]), rotate(parts[1])
    new_values = parts[2].astype(jnp.bfloat16)
    root = 1.0 / math.sqrt(LANES)
    slots = key_ref.shape[1]
    group_of = lax.broadcasted_iota(jnp.int32, (tokens, slots), 0) // steps
    scores = jnp.zeros((tokens, slots), jnp.float32)
    copies[2].wait()
    for r in range(rows):
        one = lax.dot_general(queries, key_ref[r], (((1,), (1,)), ((), ())), preferred_element_type=jnp.float32)
        scores = jnp.where(group_of == r, one, scores)
    live = lax.broadcasted_iota(jnp.int32, (tokens, slots), 1) < lens_ref[:, 0:1]
    scores = jnp.where(live, scores * root, MASKED)
    fresh = lax.dot_general(queries, new_keys, (((1,), (1,)), ((), ())), preferred_element_type=jnp.float32)
    i = lax.broadcasted_iota(jnp.int32, (tokens, tokens), 0)
    j = lax.broadcasted_iota(jnp.int32, (tokens, tokens), 1)
    causal = (i // steps == j // steps) & (j <= i)
    fresh = jnp.where(causal, fresh * root, MASKED)
    top = jnp.maximum(jnp.max(scores, axis=-1, keepdims=True), jnp.max(fresh, axis=-1, keepdims=True))
    weights = jnp.exp(scores - top)
    fresh_weights = jnp.exp(fresh - top)
    total = jnp.sum(weights, axis=-1, keepdims=True) + jnp.sum(fresh_weights, axis=-1, keepdims=True)
    mixed = jnp.dot(fresh_weights.astype(jnp.bfloat16), new_values, preferred_element_type=jnp.float32)
    copies[3].wait()
    for r in range(rows):
        own = jnp.where(group_of == r, weights, 0.0).astype(jnp.bfloat16)
        mixed = mixed + jnp.dot(own, value_ref[r], preferred_element_type=jnp.float32)
    heads = (mixed / total).astype(jnp.bfloat16)
    copies[4].wait()
    partial = jnp.dot(heads, wout_ref[...], preferred_element_type=jnp.float32)
    high = partial.astype(jnp.bfloat16)
    out_ref[0:tokens, :] = high
    out_ref[tokens:, :] = (partial - high.astype(jnp.float32)).astype(jnp.bfloat16)


def attention(message, row, tokens, gain, w_qkv, cos, sin, lens, keys, values, w_out):
    loaded = [pltpu.VMEM(a.shape, a.dtype) for a in (w_qkv, keys, values, w_out)]
    return pl.pallas_call(
        functools.partial(attention_kernel, row),
        out_shape=jax.ShapeDtypeStruct((2 * tokens, GROUP * LANES), jnp.bfloat16),
        in_specs=[hbm(), vmem(), hbm(), vmem(), vmem(), vmem(), hbm(), hbm(), hbm()],
        out_specs=vmem(),
        scratch_shapes=[pltpu.VMEM((GROUP, tokens, LANES), jnp.bfloat16)]
        + loaded
        + [pltpu.VMEM((tokens, GROUP * LANES), jnp.bfloat16), pltpu.SemaphoreType.DMA((5,))],
        compiler_params=pltpu.CompilerParams(vmem_limit_bytes=62 << 20),
        cost_estimate=pl.CostEstimate(flops=4 * 10**8, bytes_accessed=9 << 20, transcendentals=40000),
        name="attention",
    )(message, gain, w_qkv, cos, sin, lens, keys, values, w_out)


def combine_kernel(first, base, message_ref, *refs):
    scored, (out_ref, buf, payload, sem) = refs[:-4], refs[-4:]
    tokens = buf.shape[1] // 2
    copy = pltpu.make_async_copy(message_ref.at[:, pl.ds(first, 2 * tokens), :], buf, sem.at[0])
    copy.start()
    payload[tokens:, :] = jnp.zeros((payload.shape[0] - tokens, LANES), jnp.float32)
    for i, part in enumerate(scored):
        at = tokens + i * base
        payload[at : at + part.shape[0], :] = part[...]
    copy.wait()
    total = jnp.zeros((tokens, LANES), jnp.float32)
    for s in range(GROUP):
        total = total + (buf[s, 0:tokens, :].astype(jnp.float32) + buf[s, tokens:, :].astype(jnp.float32))
    payload[0:tokens, :] = total.astype(jnp.bfloat16).astype(jnp.float32)
    for d in range(GROUP):
        pltpu.make_async_copy(payload, out_ref.at[d], sem.at[1]).start()
    pltpu.make_async_copy(out_ref, out_ref, sem.at[1]).wait()


def combine(message, first, base, tokens, scored):
    rows = tokens + 2 * base
    return pl.pallas_call(
        functools.partial(combine_kernel, first, base),
        out_shape=jax.ShapeDtypeStruct((GROUP, rows, LANES), jnp.float32),
        in_specs=[hbm()] + [vmem()] * len(scored),
        out_specs=pl.BlockSpec(memory_space=pltpu.HBM),
        scratch_shapes=[
            pltpu.VMEM((GROUP, 2 * tokens, LANES), jnp.bfloat16),
            pltpu.VMEM((rows, LANES), jnp.float32),
            pltpu.SemaphoreType.DMA((2,)),
        ],
        compiler_params=pltpu.CompilerParams(vmem_limit_bytes=62 << 20),
        cost_estimate=pl.CostEstimate(flops=10**5, bytes_accessed=1 << 19, transcendentals=0),
        name="combine",
    )(message, *scored)


def score_kernel(slots, place_ref, x_hbm, *refs):
    w_hbm, (gain_ref, bias_ref, score_ref, out_ref) = refs[:10], refs[10:14]
    x_buf, w_buf, normed_ref, total_ref, x_sem, w_sems = refs[14:]
    width = GROUP * LANES
    rows = slots * LANES
    x_copy = pltpu.make_async_copy(x_hbm.at[:, pl.ds(0, rows), :], x_buf, x_sem.at[0])
    x_copy.start()
    core, x, z = place_ref[0], place_ref[1], place_ref[2]
    for side in range(2):
        owner = core if side == 0 else 1 - core
        near = jnp.where(owner == 0, z, x)
        far = jnp.where(owner == 0, x, z)
        for index, (step, firsts) in enumerate(RECEIVED):
            last = (far + step) & 3
            for row, a in enumerate(firsts):
                mine = (near + NEAR[a]) & 3
                block = jnp.where(owner == 0, last * 4 + mine, mine * 4 + last)
                pltpu.make_async_copy(
                    w_hbm[side * 5 + index].at[pl.ds(row * SPAN, SPAN), :],
                    w_buf.at[owner, pl.ds(pl.multiple_of(block * SPAN, SPAN), SPAN), :],
                    w_sems.at[owner],
                ).start()
    x_copy.wait()

    @pl.loop(0, slots)
    def _(q):
        here = pl.ds(pl.multiple_of(q * LANES, LANES), LANES)

        def square(c, squares):
            for i in range(CHUNK):
                part = x_buf[c * CHUNK + i, here, :].astype(jnp.float32)
                squares = squares + part * part
            return squares

        squares = lax.fori_loop(0, GROUP // CHUNK, square, jnp.zeros((LANES, LANES), jnp.float32))
        mean = jnp.sum(squares, axis=-1, keepdims=True) / width
        inverse_rms = lax.rsqrt(mean + EPS)

        @pl.loop(0, GROUP // CHUNK)
        def _(c):
            for i in range(CHUNK):
                s = c * CHUNK + i
                part = x_buf[s, here, :].astype(jnp.float32) * inverse_rms * gain_ref[pl.ds(s, 1), :]
                normed_ref[here, pl.ds(pl.multiple_of(s * LANES, LANES), LANES)] = part.astype(jnp.bfloat16)

    total_ref[...] = jnp.zeros_like(total_ref)

    @pl.loop(0, 4)
    def _(i):
        owner = jnp.where(i < 2, core, 1 - core)
        h = i & 1

        @pl.when(h == 0)
        def _():
            pltpu.make_async_copy(w_buf.at[owner], w_buf.at[owner], w_sems.at[owner]).wait()

        bias, score = bias_ref[pl.ds(owner * 2 + h, 1), :], score_ref[pl.ds(owner * 2 + h, 1), :]
        w = w_buf[owner, :, pl.ds(pl.multiple_of(h * COLS, COLS), COLS)]
        for part in range(0, rows, HALF):
            some = slice(part, min(part + HALF, rows))
            pre = jnp.dot(normed_ref[some, :], w, preferred_element_type=jnp.float32) + bias
            hidden = pre / (1.0 + jnp.exp(-pre)) * score
            total = total_ref[some, :]
            for c in range(COLS // LANES):
                total = total + hidden[:, c * LANES : (c + 1) * LANES]
            total_ref[some, :] = total

    for q in range(slots):
        out_ref[q : q + 1, :] = jnp.sum(total_ref[q * LANES : (q + 1) * LANES, :].T, axis=0, keepdims=True)


def score_rows(message, slots, place, parts, gain, bias, w_score):
    width = GROUP * LANES
    rows = slots * LANES
    return pl.pallas_call(
        functools.partial(score_kernel, slots),
        out_shape=jax.ShapeDtypeStruct((slots, LANES), jnp.float32),
        in_specs=[pl.BlockSpec(memory_space=pltpu.SMEM)] + [hbm()] * 11 + [vmem()] * 3,
        out_specs=vmem(),
        scratch_shapes=[
            pltpu.VMEM((GROUP, rows, LANES), jnp.bfloat16),
            pltpu.VMEM((2, width, 2 * COLS), jnp.bfloat16),
            pltpu.VMEM((rows, width), jnp.bfloat16),
            pltpu.VMEM((rows, LANES), jnp.float32),
            pltpu.SemaphoreType.DMA((1,)),
            pltpu.SemaphoreType.DMA((2,)),
        ],
        compiler_params=pltpu.CompilerParams(vmem_limit_bytes=62 << 20),
        cost_estimate=pl.CostEstimate(
            flops=2 * rows * width * 4 * COLS, bytes_accessed=24 << 20, transcendentals=rows * 4 * COLS
        ),
        name="score",
    )(place, message, *parts, gain, bias, w_score)


def block_starts(lens_ref, pieces):
    starts, counts = [], []
    start = 0
    for i in range(pieces):
        count = lax.shift_right_logical(lens_ref[i] + (LANES - 1), 7)
        starts.append(start)
        counts.append(count)
        start = start + count
    return starts, counts


def pack_kernel(pieces, first, slots, lens_ref, pieces_ref, *refs):
    starts, _ = block_starts(lens_ref, pieces)
    blocks = pieces_ref.shape[1] // LANES
    rows = slots * LANES
    if first:
        partial_ref, out_ref, stage, in_sems, out_sem = refs
        extra = partial_ref.shape[0]
    else:
        ids_ref, table_ref, out_ref, stage, tiles, picked, in_sems, out_sem = refs
        tokens = ids_ref.shape[0] * ids_ref.shape[1]
        steps = ids_ref.shape[1]
        for i in range(tokens):
            above = lax.shift_right_logical(ids_ref[i // steps, i % steps], 3) * 8
            pltpu.make_async_copy(table_ref.at[pl.ds(pl.multiple_of(above, 8), 8), :], tiles.at[i], in_sems.at[4]).start()
    chunk = GROUP // 4
    for c in range(4):

        @pl.loop(c * chunk, (c + 1) * chunk)
        def _(d):
            for q in range(slots):
                slot = (first + q) * GROUP + d
                piece, start = 0, 0
                for i in range(1, pieces):
                    after = slot >= starts[i]
                    piece = jnp.where(after, i, piece)
                    start = jnp.where(after, starts[i], start)
                block = jnp.minimum(slot - start, blocks - 1)
                pltpu.make_async_copy(
                    pieces_ref.at[piece, pl.ds(pl.multiple_of(block * LANES, LANES), LANES), :],
                    stage.at[d, pl.ds(q * LANES, LANES), :],
                    in_sems.at[c],
                ).start()
            if first:
                source = partial_ref.at[:, pl.ds(pl.multiple_of(d * LANES, LANES), LANES)]
                pltpu.make_async_copy(source, stage.at[d, pl.ds(rows, extra), :], in_sems.at[c]).start()

    if not first:
        pltpu.make_async_copy(tiles, tiles, in_sems.at[4]).wait()
        sublane = lax.broadcasted_iota(jnp.int32, (8, LANES), 0)
        for i in range(tokens):
            own = sublane == (ids_ref[i // steps, i % steps] & 7)
            picked[i : i + 1, :] = jnp.sum(jnp.where(own, tiles[i].astype(jnp.float32), 0.0), axis=0, keepdims=True)
        block = picked[...].astype(jnp.bfloat16)
        for d in range(GROUP):
            stage[d, rows:, :] = block
    done = stage.shape[1] if first else rows
    for c in range(4):
        part = pl.ds(c * chunk, chunk)
        landed = stage.at[part, pl.ds(0, done), :]
        pltpu.make_async_copy(landed, landed, in_sems.at[c]).wait()
        pltpu.make_async_copy(stage.at[part], out_ref.at[part], out_sem.at[c]).start()
    for c in range(4):
        part = pl.ds(c * chunk, chunk)
        pltpu.make_async_copy(stage.at[part], out_ref.at[part], out_sem.at[c]).wait()


def pack(first, slots, extra, name, scratch, operands, specs):
    rows = slots * LANES + extra
    return pl.pallas_call(
        functools.partial(pack_kernel, operands[1].shape[0], first, slots),
        out_shape=jax.ShapeDtypeStruct((GROUP, rows, LANES), jnp.bfloat16),
        in_specs=[pl.BlockSpec(memory_space=pltpu.SMEM), hbm()] + specs,
        out_specs=pl.BlockSpec(memory_space=pltpu.HBM),
        scratch_shapes=[pltpu.VMEM((GROUP, rows, LANES), jnp.bfloat16)]
        + scratch
        + [pltpu.SemaphoreType.DMA((5,)), pltpu.SemaphoreType.DMA((4,))],
        compiler_params=pltpu.CompilerParams(vmem_limit_bytes=62 << 20),
        cost_estimate=pl.CostEstimate(flops=0, bytes_accessed=4 * GROUP * rows * LANES, transcendentals=0),
        name=name,
    )(*operands)


def pack_first(slots, piece_lens, pieces, step_ids, embed_table):
    tokens = step_ids.shape[0] * step_ids.shape[1]
    scratch = [pltpu.VMEM((tokens, 8, LANES), jnp.bfloat16), pltpu.VMEM((tokens, LANES), jnp.float32)]
    specs = [pl.BlockSpec(memory_space=pltpu.SMEM), hbm()]
    return pack(0, slots, tokens, "pack_first", scratch, (piece_lens, pieces, step_ids, embed_table), specs)


def pack_rest(first, slots, piece_lens, pieces, partial):
    return pack(first, slots, partial.shape[0], "pack_rest", [], (piece_lens, pieces, partial), [hbm()])


def finish_kernel(pieces, tokens, scalars_ref, offset_ref, result_ref, attn_ref, value_ref):
    starts, counts = block_starts(scalars_ref, pieces)
    me = scalars_ref[pieces]
    where = me * LANES + lax.broadcasted_iota(jnp.int32, (1, LANES), 1)
    for i in range(pieces):
        slot = jnp.minimum(starts[i] + jnp.minimum(me, counts[i]), pieces * GROUP - 1)
        row = result_ref[slot & (GROUP - 1), pl.ds(tokens + lax.shift_right_logical(slot, 5), 1), :]
        value_ref[i : i + 1, :] = jnp.where(where < scalars_ref[i], row + offset_ref[0], 0.0)
    rows, steps, _ = attn_ref.shape
    for s in range(GROUP):
        block = result_ref[s, 0:tokens, :].reshape(rows, steps, LANES)
        attn_ref[:, :, s * LANES : (s + 1) * LANES] = block.astype(jnp.bfloat16)


def finish(scalars, offset, result, pieces, rows, steps):
    tokens = rows * steps
    return pl.pallas_call(
        functools.partial(finish_kernel, pieces, tokens),
        out_shape=(
            jax.ShapeDtypeStruct((rows, steps, GROUP * LANES), jnp.bfloat16),
            jax.ShapeDtypeStruct((pieces, LANES), jnp.float32),
        ),
        in_specs=[pl.BlockSpec(memory_space=pltpu.SMEM)] * 2 + [vmem()],
        out_specs=(vmem(), vmem()),
        compiler_params=pltpu.CompilerParams(vmem_limit_bytes=16 << 20),
        name="finish",
    )(scalars, offset, result)


def exchange(message):
    return lax.all_to_all(message, MP, 0, 0)


def shift(value, stage, step):
    pairs = []
    for core in range(2):
        for x in range(4):
            for z in range(4):
                along_x = core != stage
                to = ((x + step) % 4 if along_x else x) * 4 + (z if along_x else (z + step) % 4)
                pairs.append((core * 16 + x * 4 + z, core * 16 + to))
    return lax.ppermute(value, ("core", "x", "z"), pairs)


def around(value, stage):
    half = value.shape[0] // 2
    right, left = shift(value, stage, 1), shift(value, stage, -1)
    return (value, right, left, shift(right[:half], stage, 1), shift(left[half:], stage, -1))


def gather_layer(w_value, *others):
    columns = w_value.shape[1] // 2
    own = lax.dynamic_slice_in_dim(w_value, lax.axis_index("core") * columns, columns, axis=1)
    other = lax.ppermute(own, "ylo", [(0, 1), (1, 0)])
    other, *others = lax.optimization_barrier((other, *others))
    even = lax.axis_index("ylo") == 0
    pair = jnp.concatenate([jnp.where(even, own, other), jnp.where(even, other, own)], axis=0)
    mine = around(jnp.concatenate(around(pair, 0), axis=0), 1)
    return mine, tuple(swap_cores(part) for part in mine[:3]), *others


def swap_cores(part):
    return lax.ppermute(part, "core", [(0, 1), (1, 0)])


def per_device(
    step_ids,
    prompt_lens,
    embed_table,
    attn_gain,
    w_qkv,
    w_out,
    key_cache,
    value_cache,
    reward_pieces,
    piece_lens,
    reward_gain,
    w_value,
    b_value,
    w_score,
    b_score,
):
    rows, steps = step_ids.shape
    tokens = rows * steps
    me = lax.axis_index(MP)
    place = jnp.stack([lax.axis_index(name) for name in ("core", "x", "z")]).astype(jnp.int32)
    bias = b_value.reshape(4, COLS)
    score = w_score.reshape(4, COLS)

    half_dim = LANES // 2
    frequency = 10000.0 ** (-2.0 * jnp.arange(half_dim, dtype=jnp.float32) / (2 * half_dim))
    positions = (prompt_lens[:, None] + jnp.arange(steps, dtype=jnp.int32)[None, :]).reshape(tokens)
    angles = positions.astype(jnp.float32)[:, None] * frequency
    cos = jnp.concatenate([jnp.cos(angles)] * 2, axis=-1)
    sin = jnp.concatenate([-jnp.sin(angles), jnp.sin(angles)], axis=-1)
    lens = jnp.broadcast_to(jnp.repeat(prompt_lens, steps)[:, None], (tokens, LANES))
    pieces, length, _ = reward_pieces.shape
    total = jnp.sum((piece_lens + (LANES - 1)) // LANES)
    most = jnp.full((8, LANES), total, jnp.int32).astype(jnp.float32)
    for axis in ("core", "yhi"):
        most = jnp.maximum(most, lax.ppermute(most, axis, [(0, 1), (1, 0)]))
    base = length // LANES * pieces // GROUP // 2
    message = pack_first(base, piece_lens, reward_pieces, step_ids, embed_table)
    mine, theirs, message, most = gather_layer(w_value, message, most)
    rest = jnp.clip((most[0, 0].astype(jnp.int32) + (GROUP - 1)) // GROUP - base, 0, base)
    first = exchange(message)
    partial = attention(
        first,
        base * LANES,
        tokens,
        attn_gain.astype(jnp.float32).reshape(GROUP, LANES),
        w_qkv,
        cos,
        sin,
        lens,
        key_cache.reshape(rows, -1, LANES),
        value_cache.reshape(rows, -1, LANES),
        w_out,
    )
    gain = reward_gain.astype(jnp.float32).reshape(GROUP, LANES)

    def remainder(slots, first, partial, place, piece_lens, reward_pieces, gain, bias, score, mine, theirs):
        second = exchange(pack_rest(base, slots, piece_lens, reward_pieces, partial))
        parts = mine + theirs + tuple(swap_cores(part) for part in mine[3:])
        scored = [score_rows(first, base, place, parts, gain, bias, score)]
        if slots:
            scored.append(score_rows(second, slots, place, parts, gain, bias, score))
        return combine(second, slots * LANES, base, tokens, scored)

    payload = lax.switch(
        rest,
        [functools.partial(remainder, slots) for slots in range(base + 1)],
        first,
        partial,
        place,
        piece_lens,
        reward_pieces,
        gain,
        bias,
        score,
        mine,
        theirs,
    )
    scalars = jnp.concatenate([piece_lens, me.reshape(1).astype(jnp.int32)])
    attn_out, piece_values = finish(scalars, b_score, exchange(payload), pieces, rows, steps)
    return (attn_out, piece_values)


def solution(mesh):
    fine = Mesh(mesh.devices.reshape(2, 2, 4, 4, 2), DP + MP)
    return jax.shard_map(
        per_device,
        mesh=fine,
        in_specs=(
            P(DP, None),
            P(DP),
            P(None, MP),
            P(),
            P(None, None, MP),
            P(MP, None),
            P(DP, MP, None, None),
            P(DP, MP, None, None),
            P(DP, None, MP),
            P(DP),
            P(),
            P(MP, None),
            P(),
            P(),
            P(),
        ),
        out_specs=(P(DP, None, None), P(DP, MP)),
        check_vma=False,
    )
```

```python
import functools
import math

import jax
import jax.numpy as jnp
from jax import lax
from jax.experimental import pallas as pl
from jax.experimental.pallas import tpu as pltpu
from jax.sharding import Mesh, PartitionSpec as P


EPS = 1e-05
MASKED = -1e30
DP = ("yhi", "core")
MP = ("x", "z", "ylo")
GROUP = 32
LANES = 128
COLS = 512
HALF = 256
CHUNK = 4
RECEIVED = ((0, 0, 4), (-1, 0, 4), (1, 0, 4), (2, 0, 2), (2, 2, 4))


def vmem():
    return pl.BlockSpec(memory_space=pltpu.VMEM)


def hbm():
    return pl.BlockSpec(memory_space=pl.ANY)


def attention_kernel(row, message_ref, gain_ref, wqkv_hbm, cos_ref, sin_ref, lens_ref, key_hbm, value_hbm, wout_hbm, out_ref, *scratch):
    emb_ref, wqkv_ref, key_ref, value_ref, wout_ref, normed_ref, sems = scratch
    tokens = emb_ref.shape[1]
    copies = [
        pltpu.make_async_copy(source, target, sems.at[i])
        for i, (source, target) in enumerate(
            [
                (message_ref.at[:, pl.ds(row, tokens), :], emb_ref),
                (wqkv_hbm, wqkv_ref),
                (key_hbm, key_ref),
                (value_hbm, value_ref),
                (wout_hbm, wout_ref),
            ]
        )
    ]
    for copy in copies:
        copy.start()
    width = GROUP * LANES
    rows = key_ref.shape[0]
    steps = tokens // rows
    copies[0].wait()
    squares = jnp.zeros((tokens, LANES), jnp.float32)
    for s in range(GROUP):
        part = emb_ref[s].astype(jnp.float32)
        squares = squares + part * part
    mean = jnp.sum(squares, axis=-1, keepdims=True) / width
    inverse_rms = lax.rsqrt(mean + EPS)
    for s in range(GROUP):
        part = emb_ref[s].astype(jnp.float32) * inverse_rms * gain_ref[s : s + 1, :]
        normed_ref[:, s * LANES : (s + 1) * LANES] = part.astype(jnp.bfloat16)
    normed = normed_ref[...]
    copies[1].wait()
    parts = [jnp.dot(normed, wqkv_ref[c], preferred_element_type=jnp.float32) for c in range(3)]
    cos, sin = cos_ref[...], sin_ref[...]
    half = LANES // 2

    def rotate(v):
        return (v * cos + pltpu.roll(v, half, 1) * sin).astype(jnp.bfloat16)

    queries, new_keys = rotate(parts[0]), rotate(parts[1])
    new_values = parts[2].astype(jnp.bfloat16)
    root = 1.0 / math.sqrt(LANES)
    slots = key_ref.shape[1]
    group_of = lax.broadcasted_iota(jnp.int32, (tokens, slots), 0) // steps
    scores = jnp.zeros((tokens, slots), jnp.float32)
    copies[2].wait()
    for r in range(rows):
        one = lax.dot_general(queries, key_ref[r], (((1,), (1,)), ((), ())), preferred_element_type=jnp.float32)
        scores = jnp.where(group_of == r, one, scores)
    live = lax.broadcasted_iota(jnp.int32, (tokens, slots), 1) < lens_ref[:, 0:1]
    scores = jnp.where(live, scores * root, MASKED)
    fresh = lax.dot_general(queries, new_keys, (((1,), (1,)), ((), ())), preferred_element_type=jnp.float32)
    i = lax.broadcasted_iota(jnp.int32, (tokens, tokens), 0)
    j = lax.broadcasted_iota(jnp.int32, (tokens, tokens), 1)
    causal = (i // steps == j // steps) & (j <= i)
    fresh = jnp.where(causal, fresh * root, MASKED)
    top = jnp.maximum(jnp.max(scores, axis=-1, keepdims=True), jnp.max(fresh, axis=-1, keepdims=True))
    weights = jnp.exp(scores - top)
    fresh_weights = jnp.exp(fresh - top)
    total = jnp.sum(weights, axis=-1, keepdims=True) + jnp.sum(fresh_weights, axis=-1, keepdims=True)
    mixed = jnp.dot(fresh_weights.astype(jnp.bfloat16), new_values, preferred_element_type=jnp.float32)
    copies[3].wait()
    for r in range(rows):
        own = jnp.where(group_of == r, weights, 0.0).astype(jnp.bfloat16)
        mixed = mixed + jnp.dot(own, value_ref[r], preferred_element_type=jnp.float32)
    heads = (mixed / total).astype(jnp.bfloat16)
    copies[4].wait()
    partial = jnp.dot(heads, wout_ref[...], preferred_element_type=jnp.float32)
    high = partial.astype(jnp.bfloat16)
    out_ref[0:tokens, :] = high
    out_ref[tokens:, :] = (partial - high.astype(jnp.float32)).astype(jnp.bfloat16)


def attention(message, row, tokens, gain, w_qkv, cos, sin, lens, keys, values, w_out):
    loaded = [pltpu.VMEM(a.shape, a.dtype) for a in (w_qkv, keys, values, w_out)]
    return pl.pallas_call(
        functools.partial(attention_kernel, row),
        out_shape=jax.ShapeDtypeStruct((2 * tokens, GROUP * LANES), jnp.bfloat16),
        in_specs=[hbm(), vmem(), hbm(), vmem(), vmem(), vmem(), hbm(), hbm(), hbm()],
        out_specs=vmem(),
        scratch_shapes=[pltpu.VMEM((GROUP, tokens, LANES), jnp.bfloat16)]
        + loaded
        + [pltpu.VMEM((tokens, GROUP * LANES), jnp.bfloat16), pltpu.SemaphoreType.DMA((5,))],
        compiler_params=pltpu.CompilerParams(vmem_limit_bytes=62 << 20),
        cost_estimate=pl.CostEstimate(flops=4 * 10**8, bytes_accessed=9 << 20, transcendentals=40000),
        name="attention",
    )(message, gain, w_qkv, cos, sin, lens, keys, values, w_out)


def combine_kernel(first, base, message_ref, *refs):
    scored, (out_ref, buf, payload, sem) = refs[:-4], refs[-4:]
    tokens = buf.shape[1] // 2
    copy = pltpu.make_async_copy(message_ref.at[:, pl.ds(first, 2 * tokens), :], buf, sem.at[0])
    copy.start()
    payload[tokens:, :] = jnp.zeros((payload.shape[0] - tokens, LANES), jnp.float32)
    for i, part in enumerate(scored):
        at = tokens + i * base
        payload[at : at + part.shape[0], :] = part[...]
    copy.wait()
    total = jnp.zeros((tokens, LANES), jnp.float32)
    for s in range(GROUP):
        total = total + (buf[s, 0:tokens, :].astype(jnp.float32) + buf[s, tokens:, :].astype(jnp.float32))
    payload[0:tokens, :] = total.astype(jnp.bfloat16).astype(jnp.float32)
    for d in range(GROUP):
        pltpu.make_async_copy(payload, out_ref.at[d], sem.at[1]).start()
    pltpu.make_async_copy(out_ref, out_ref, sem.at[1]).wait()


def combine(message, first, base, tokens, scored):
    rows = tokens + 2 * base
    return pl.pallas_call(
        functools.partial(combine_kernel, first, base),
        out_shape=jax.ShapeDtypeStruct((GROUP, rows, LANES), jnp.float32),
        in_specs=[hbm()] + [vmem()] * len(scored),
        out_specs=pl.BlockSpec(memory_space=pltpu.HBM),
        scratch_shapes=[
            pltpu.VMEM((GROUP, 2 * tokens, LANES), jnp.bfloat16),
            pltpu.VMEM((rows, LANES), jnp.float32),
            pltpu.SemaphoreType.DMA((2,)),
        ],
        compiler_params=pltpu.CompilerParams(vmem_limit_bytes=62 << 20),
        cost_estimate=pl.CostEstimate(flops=10**5, bytes_accessed=1 << 19, transcendentals=0),
        name="combine",
    )(message, *scored)


def score_kernel(slots, place_ref, x_hbm, *refs):
    w_hbm, (gain_ref, bias_ref, score_ref, out_ref) = refs[:20], refs[20:24]
    x_buf, w_buf, normed_ref, total_ref, x_sem, w_sems = refs[24:]
    width = GROUP * LANES
    rows = slots * LANES
    x_copy = pltpu.make_async_copy(x_hbm.at[:, pl.ds(0, rows), :], x_buf, x_sem.at[0])
    x_copy.start()
    core, x, z, ylo = place_ref[0], place_ref[1], place_ref[2], place_ref[3]
    for side in range(2):
        owner = core if side == 0 else 1 - core
        near = jnp.where(owner == 0, z, x)
        far = jnp.where(owner == 0, x, z)
        for index, (step, begin, end) in enumerate(RECEIVED + RECEIVED):
            last = (far + step) & 3
            low = ylo if index < len(RECEIVED) else 1 - ylo

            @pl.loop(begin, end)
            def _(a):
                mine = (near + jnp.where(a < 2, -a, a - 1)) & 3
                block = jnp.where(owner == 0, last * 4 + mine, mine * 4 + last) * 2 + low
                pltpu.make_async_copy(
                    w_hbm[side * 10 + index].at[pl.ds(pl.multiple_of((a - begin) * LANES, LANES), LANES), :],
                    w_buf.at[owner, pl.ds(pl.multiple_of(block * LANES, LANES), LANES), :],
                    w_sems.at[owner],
                ).start()

    x_copy.wait()

    @pl.loop(0, slots)
    def _(q):
        here = pl.ds(pl.multiple_of(q * LANES, LANES), LANES)

        def square(c, squares):
            for i in range(CHUNK):
                part = x_buf[c * CHUNK + i, here, :].astype(jnp.float32)
                squares = squares + part * part
            return squares

        squares = lax.fori_loop(0, GROUP // CHUNK, square, jnp.zeros((LANES, LANES), jnp.float32))
        mean = jnp.sum(squares, axis=-1, keepdims=True) / width
        inverse_rms = lax.rsqrt(mean + EPS)

        @pl.loop(0, GROUP // CHUNK)
        def _(c):
            for i in range(CHUNK):
                s = c * CHUNK + i
                part = x_buf[s, here, :].astype(jnp.float32) * inverse_rms * gain_ref[pl.ds(s, 1), :]
                normed_ref[here, pl.ds(pl.multiple_of(s * LANES, LANES), LANES)] = part.astype(jnp.bfloat16)

    total_ref[...] = jnp.zeros_like(total_ref)

    @pl.loop(0, 4)
    def _(i):
        owner = jnp.where(i < 2, core, 1 - core)
        h = i & 1

        @pl.when(h == 0)
        def _():
            pltpu.make_async_copy(w_buf.at[owner], w_buf.at[owner], w_sems.at[owner]).wait()

        bias, score = bias_ref[pl.ds(owner * 2 + h, 1), :], score_ref[pl.ds(owner * 2 + h, 1), :]
        w = w_buf[owner, :, pl.ds(pl.multiple_of(h * COLS, COLS), COLS)]
        for part in range(0, rows, HALF):
            some = slice(part, min(part + HALF, rows))
            pre = jnp.dot(normed_ref[some, :], w, preferred_element_type=jnp.float32) + bias
            hidden = pre / (1.0 + jnp.exp(-pre)) * score
            total = total_ref[some, :]
            for c in range(COLS // LANES):
                total = total + hidden[:, c * LANES : (c + 1) * LANES]
            total_ref[some, :] = total

    for q in range(slots):
        out_ref[q : q + 1, :] = jnp.sum(total_ref[q * LANES : (q + 1) * LANES, :].T, axis=0, keepdims=True)


def score_rows(message, slots, place, parts, gain, bias, w_score):
    width = GROUP * LANES
    rows = slots * LANES
    return pl.pallas_call(
        functools.partial(score_kernel, slots),
        out_shape=jax.ShapeDtypeStruct((slots, LANES), jnp.float32),
        in_specs=[pl.BlockSpec(memory_space=pltpu.SMEM)] + [hbm()] * 21 + [vmem()] * 3,
        out_specs=vmem(),
        scratch_shapes=[
            pltpu.VMEM((GROUP, rows, LANES), jnp.bfloat16),
            pltpu.VMEM((2, width, 2 * COLS), jnp.bfloat16),
            pltpu.VMEM((rows, width), jnp.bfloat16),
            pltpu.VMEM((rows, LANES), jnp.float32),
            pltpu.SemaphoreType.DMA((1,)),
            pltpu.SemaphoreType.DMA((2,)),
        ],
        compiler_params=pltpu.CompilerParams(vmem_limit_bytes=62 << 20),
        cost_estimate=pl.CostEstimate(
            flops=2 * rows * width * 4 * COLS, bytes_accessed=24 << 20, transcendentals=rows * 4 * COLS
        ),
        name="score",
    )(place, message, *parts, gain, bias, w_score)


def block_starts(lens_ref, pieces):
    starts, counts = [], []
    start = 0
    for i in range(pieces):
        count = lax.shift_right_logical(lens_ref[i] + (LANES - 1), 7)
        starts.append(start)
        counts.append(count)
        start = start + count
    return starts, counts


def pack_kernel(pieces, first, slots, lens_ref, pieces_ref, *refs):
    starts, _ = block_starts(lens_ref, pieces)
    blocks = pieces_ref.shape[1] // LANES
    rows = slots * LANES
    if first:
        partial_ref, out_ref, stage, in_sems, out_sem = refs
        extra = partial_ref.shape[0]
    else:
        ids_ref, table_ref, out_ref, stage, tiles, picked, in_sems, out_sem = refs
        tokens = ids_ref.shape[0] * ids_ref.shape[1]
        steps = ids_ref.shape[1]
        for i in range(tokens):
            above = lax.shift_right_logical(ids_ref[i // steps, i % steps], 3) * 8
            pltpu.make_async_copy(table_ref.at[pl.ds(pl.multiple_of(above, 8), 8), :], tiles.at[i], in_sems.at[4]).start()
    chunk = GROUP // 4

    @pl.loop(0, GROUP)
    def _(d):
        sem = in_sems.at[d // chunk]

        @pl.loop(0, slots)
        def _(q):
            slot = (first + q) * GROUP + d
            piece, start = 0, 0
            for i in range(1, pieces):
                after = slot >= starts[i]
                piece = jnp.where(after, i, piece)
                start = jnp.where(after, starts[i], start)
            block = jnp.minimum(slot - start, blocks - 1)
            pltpu.make_async_copy(
                pieces_ref.at[piece, pl.ds(pl.multiple_of(block * LANES, LANES), LANES), :],
                stage.at[d, pl.ds(pl.multiple_of(q * LANES, LANES), LANES), :],
                sem,
            ).start()

        if first:
            source = partial_ref.at[:, pl.ds(pl.multiple_of(d * LANES, LANES), LANES)]
            pltpu.make_async_copy(source, stage.at[d, pl.ds(rows, extra), :], sem).start()

    if not first:
        pltpu.make_async_copy(tiles, tiles, in_sems.at[4]).wait()
        sublane = lax.broadcasted_iota(jnp.int32, (8, LANES), 0)
        for i in range(tokens):
            own = sublane == (ids_ref[i // steps, i % steps] & 7)
            picked[i : i + 1, :] = jnp.sum(jnp.where(own, tiles[i].astype(jnp.float32), 0.0), axis=0, keepdims=True)
        block = picked[...].astype(jnp.bfloat16)
        for d in range(GROUP):
            stage[d, rows:, :] = block
    done = stage.shape[1] if first else rows
    for c in range(4):
        part = pl.ds(c * chunk, chunk)
        landed = stage.at[part, pl.ds(0, done), :]
        pltpu.make_async_copy(landed, landed, in_sems.at[c]).wait()
        pltpu.make_async_copy(stage.at[part], out_ref.at[part], out_sem.at[c]).start()
    for c in range(4):
        part = pl.ds(c * chunk, chunk)
        pltpu.make_async_copy(stage.at[part], out_ref.at[part], out_sem.at[c]).wait()


def pack(first, slots, extra, scratch, operands, specs):
    rows = slots * LANES + extra
    return pl.pallas_call(
        functools.partial(pack_kernel, operands[1].shape[0], first, slots),
        out_shape=jax.ShapeDtypeStruct((GROUP, rows, LANES), jnp.bfloat16),
        in_specs=[pl.BlockSpec(memory_space=pltpu.SMEM), hbm()] + specs,
        out_specs=pl.BlockSpec(memory_space=pltpu.HBM),
        scratch_shapes=[pltpu.VMEM((GROUP, rows, LANES), jnp.bfloat16)]
        + scratch
        + [pltpu.SemaphoreType.DMA((5,)), pltpu.SemaphoreType.DMA((4,))],
        compiler_params=pltpu.CompilerParams(vmem_limit_bytes=62 << 20),
        cost_estimate=pl.CostEstimate(flops=0, bytes_accessed=4 * GROUP * rows * LANES, transcendentals=0),
    )(*operands)


def pack_first(slots, piece_lens, pieces, step_ids, embed_table):
    tokens = step_ids.shape[0] * step_ids.shape[1]
    scratch = [pltpu.VMEM((tokens, 8, LANES), jnp.bfloat16), pltpu.VMEM((tokens, LANES), jnp.float32)]
    specs = [pl.BlockSpec(memory_space=pltpu.SMEM), hbm()]
    return pack(0, slots, tokens, scratch, (piece_lens, pieces, step_ids, embed_table), specs)


def pack_rest(first, slots, piece_lens, pieces, partial):
    return pack(first, slots, partial.shape[0], [], (piece_lens, pieces, partial), [hbm()])


def finish_kernel(pieces, tokens, scalars_ref, offset_ref, result_ref, attn_ref, value_ref):
    starts, counts = block_starts(scalars_ref, pieces)
    me = scalars_ref[pieces]
    where = me * LANES + lax.broadcasted_iota(jnp.int32, (1, LANES), 1)
    for i in range(pieces):
        slot = jnp.minimum(starts[i] + jnp.minimum(me, counts[i]), pieces * GROUP - 1)
        row = result_ref[slot & (GROUP - 1), pl.ds(tokens + lax.shift_right_logical(slot, 5), 1), :]
        value_ref[i : i + 1, :] = jnp.where(where < scalars_ref[i], row + offset_ref[0], 0.0)
    rows, steps, _ = attn_ref.shape
    for s in range(GROUP):
        block = result_ref[s, 0:tokens, :].reshape(rows, steps, LANES)
        attn_ref[:, :, s * LANES : (s + 1) * LANES] = block.astype(jnp.bfloat16)


def finish(scalars, offset, result, pieces, rows, steps):
    tokens = rows * steps
    return pl.pallas_call(
        functools.partial(finish_kernel, pieces, tokens),
        out_shape=(
            jax.ShapeDtypeStruct((rows, steps, GROUP * LANES), jnp.bfloat16),
            jax.ShapeDtypeStruct((pieces, LANES), jnp.float32),
        ),
        in_specs=[pl.BlockSpec(memory_space=pltpu.SMEM)] * 2 + [vmem()],
        out_specs=(vmem(), vmem()),
        compiler_params=pltpu.CompilerParams(vmem_limit_bytes=16 << 20),
        name="finish",
    )(scalars, offset, result)


def exchange(message):
    return lax.all_to_all(message, MP, 0, 0)


def shift(value, stage, step):
    pairs = []
    for core in range(2):
        for x in range(4):
            for z in range(4):
                along_x = core != stage
                to = ((x + step) % 4 if along_x else x) * 4 + (z if along_x else (z + step) % 4)
                pairs.append((core * 16 + x * 4 + z, core * 16 + to))
    return lax.ppermute(value, ("core", "x", "z"), pairs)


def around(value, stage):
    half = value.shape[0] // 2
    right, left = shift(value, stage, 1), shift(value, stage, -1)
    return (value, right, left, shift(right[:half], stage, 1), shift(left[half:], stage, -1))


def across(value, pairs):
    return lax.ppermute(value, ("yhi", "ylo"), [pair for i, j in pairs for pair in ((i, j), (j, i))])


def gather_layer(w_value, message, most):
    columns = w_value.shape[1] // 2
    own = lax.dynamic_slice_in_dim(w_value, lax.axis_index("core") * columns, columns, axis=1)
    plane = jnp.concatenate(around(own, 0), axis=0)
    half = plane.shape[0] // 2
    right, left = shift(plane, 1, 1), shift(plane, 1, -1)
    ahead, behind, message, most = lax.optimization_barrier((right[:half], left[half:], message, most))
    near = (plane, right, left)
    ahead = shift(ahead, 1, 1)
    behind = shift(behind, 1, -1)
    rest = (ahead, behind)
    outer, inner = ((1, 2), (3, 0)), ((0, 1), (2, 3))
    others = (across(plane, outer),)
    others += (across(right, outer), across(left, outer)) + tuple(across(v, inner) for v in rest)
    mine = near + rest + others
    return mine + tuple(lax.ppermute(v, "core", [(0, 1), (1, 0)]) for v in mine), message, most


def per_device(
    step_ids,
    prompt_lens,
    embed_table,
    attn_gain,
    w_qkv,
    w_out,
    key_cache,
    value_cache,
    reward_pieces,
    piece_lens,
    reward_gain,
    w_value,
    b_value,
    w_score,
    b_score,
):
    rows, steps = step_ids.shape
    tokens = rows * steps
    me = lax.axis_index(MP)
    place = jnp.stack([lax.axis_index(name) for name in ("core", "x", "z", "ylo")]).astype(jnp.int32)
    bias = b_value.reshape(4, COLS)
    score = w_score.reshape(4, COLS)

    half_dim = LANES // 2
    frequency = 10000.0 ** (-2.0 * jnp.arange(half_dim, dtype=jnp.float32) / (2 * half_dim))
    positions = (prompt_lens[:, None] + jnp.arange(steps, dtype=jnp.int32)[None, :]).reshape(tokens)
    angles = positions.astype(jnp.float32)[:, None] * frequency
    cos = jnp.concatenate([jnp.cos(angles)] * 2, axis=-1)
    sin = jnp.concatenate([-jnp.sin(angles), jnp.sin(angles)], axis=-1)
    lens = jnp.broadcast_to(jnp.repeat(prompt_lens, steps)[:, None], (tokens, LANES))
    pieces, length, _ = reward_pieces.shape
    total = jnp.sum((piece_lens + (LANES - 1)) // LANES)
    most = jnp.full((8, LANES), total, jnp.int32).astype(jnp.float32)
    for axis in ("core", "yhi"):
        most = jnp.maximum(most, lax.ppermute(most, axis, [(0, 1), (1, 0)]))
    base = length // LANES * pieces // GROUP // 2
    message = pack_first(base, piece_lens, reward_pieces, step_ids, embed_table)
    parts, message, most = gather_layer(w_value, message, most)
    rest = jnp.clip((most[0, 0].astype(jnp.int32) + (GROUP - 1)) // GROUP - base, 0, base)
    first = exchange(message)
    partial = attention(
        first,
        base * LANES,
        tokens,
        attn_gain.astype(jnp.float32).reshape(GROUP, LANES),
        w_qkv,
        cos,
        sin,
        lens,
        key_cache.reshape(rows, -1, LANES),
        value_cache.reshape(rows, -1, LANES),
        w_out,
    )
    gain = reward_gain.astype(jnp.float32).reshape(GROUP, LANES)

    def remainder(slots, first, partial, place, piece_lens, reward_pieces, gain, bias, score, parts):
        second = exchange(pack_rest(base, slots, piece_lens, reward_pieces, partial))
        scored = [score_rows(first, base, place, parts, gain, bias, score)]
        if slots:
            scored.append(score_rows(second, slots, place, parts, gain, bias, score))
        return combine(second, slots * LANES, base, tokens, scored)

    payload = lax.switch(
        rest,
        [functools.partial(remainder, slots) for slots in range(base + 1)],
        first,
        partial,
        place,
        piece_lens,
        reward_pieces,
        gain,
        bias,
        score,
        parts,
    )
    scalars = jnp.concatenate([piece_lens, me.reshape(1).astype(jnp.int32)])
    attn_out, piece_values = finish(scalars, b_score, exchange(payload), pieces, rows, steps)
    return (attn_out, piece_values)


def solution(mesh):
    fine = Mesh(mesh.devices.reshape(2, 2, 4, 4, 2), DP + MP)
    return jax.shard_map(
        per_device,
        mesh=fine,
        in_specs=(
            P(DP, None),
            P(DP),
            P(None, MP),
            P(),
            P(None, None, MP),
            P(MP, None),
            P(DP, MP, None, None),
            P(DP, MP, None, None),
            P(DP, None, MP),
            P(DP),
            P(),
            P(MP, None),
            P(),
            P(),
            P(),
        ),
        out_specs=(P(DP, None, None), P(DP, MP)),
        check_vma=False,
    )
```

```python
import functools
import math

import jax
import jax.numpy as jnp
from jax import lax
from jax.experimental import pallas as pl
from jax.experimental.pallas import tpu as pltpu
from jax.sharding import Mesh, PartitionSpec as P


EPS = 1e-05
MASKED = -1e30
DP = ("yhi", "core")
MP = ("x", "z", "ylo")
GROUP = 32
LANES = 128
COLS = 512
HALF = 256
CHUNK = 4
RECEIVED = ((0, 0, 4), (-1, 0, 4), (1, 0, 4), (2, 0, 2), (2, 2, 4))


def vmem():
    return pl.BlockSpec(memory_space=pltpu.VMEM)


def hbm():
    return pl.BlockSpec(memory_space=pl.ANY)


def attention_kernel(row, message_ref, gain_ref, wqkv_hbm, cos_ref, sin_ref, lens_ref, key_hbm, value_hbm, wout_hbm, out_ref, *scratch):
    emb_ref, wqkv_ref, key_ref, value_ref, wout_ref, normed_ref, sems = scratch
    tokens = emb_ref.shape[1]
    copies = [
        pltpu.make_async_copy(source, target, sems.at[i])
        for i, (source, target) in enumerate(
            [
                (message_ref.at[:, pl.ds(row, tokens), :], emb_ref),
                (wqkv_hbm, wqkv_ref),
                (key_hbm, key_ref),
                (value_hbm, value_ref),
                (wout_hbm, wout_ref),
            ]
        )
    ]
    for copy in copies:
        copy.start()
    width = GROUP * LANES
    rows = key_ref.shape[0]
    steps = tokens // rows
    copies[0].wait()
    squares = jnp.zeros((tokens, LANES), jnp.float32)
    for s in range(GROUP):
        part = emb_ref[s].astype(jnp.float32)
        squares = squares + part * part
    mean = jnp.sum(squares, axis=-1, keepdims=True) / width
    inverse_rms = lax.rsqrt(mean + EPS)
    for s in range(GROUP):
        part = emb_ref[s].astype(jnp.float32) * inverse_rms * gain_ref[s : s + 1, :]
        normed_ref[:, s * LANES : (s + 1) * LANES] = part.astype(jnp.bfloat16)
    normed = normed_ref[...]
    copies[1].wait()
    parts = [jnp.dot(normed, wqkv_ref[c], preferred_element_type=jnp.float32) for c in range(3)]
    cos, sin = cos_ref[...], sin_ref[...]
    half = LANES // 2

    def rotate(v):
        return (v * cos + pltpu.roll(v, half, 1) * sin).astype(jnp.bfloat16)

    queries, new_keys = rotate(parts[0]), rotate(parts[1])
    new_values = parts[2].astype(jnp.bfloat16)
    root = 1.0 / math.sqrt(LANES)
    slots = key_ref.shape[1]
    group_of = lax.broadcasted_iota(jnp.int32, (tokens, slots), 0) // steps
    scores = jnp.zeros((tokens, slots), jnp.float32)
    copies[2].wait()
    for r in range(rows):
        one = lax.dot_general(queries, key_ref[r], (((1,), (1,)), ((), ())), preferred_element_type=jnp.float32)
        scores = jnp.where(group_of == r, one, scores)
    live = lax.broadcasted_iota(jnp.int32, (tokens, slots), 1) < lens_ref[:, 0:1]
    scores = jnp.where(live, scores * root, MASKED)
    fresh = lax.dot_general(queries, new_keys, (((1,), (1,)), ((), ())), preferred_element_type=jnp.float32)
    i = lax.broadcasted_iota(jnp.int32, (tokens, tokens), 0)
    j = lax.broadcasted_iota(jnp.int32, (tokens, tokens), 1)
    causal = (i // steps == j // steps) & (j <= i)
    fresh = jnp.where(causal, fresh * root, MASKED)
    top = jnp.maximum(jnp.max(scores, axis=-1, keepdims=True), jnp.max(fresh, axis=-1, keepdims=True))
    weights = jnp.exp(scores - top)
    fresh_weights = jnp.exp(fresh - top)
    total = jnp.sum(weights, axis=-1, keepdims=True) + jnp.sum(fresh_weights, axis=-1, keepdims=True)
    mixed = jnp.dot(fresh_weights.astype(jnp.bfloat16), new_values, preferred_element_type=jnp.float32)
    copies[3].wait()
    for r in range(rows):
        own = jnp.where(group_of == r, weights, 0.0).astype(jnp.bfloat16)
        mixed = mixed + jnp.dot(own, value_ref[r], preferred_element_type=jnp.float32)
    heads = (mixed / total).astype(jnp.bfloat16)
    copies[4].wait()
    partial = jnp.dot(heads, wout_ref[...], preferred_element_type=jnp.float32)
    high = partial.astype(jnp.bfloat16)
    out_ref[0:tokens, :] = high
    out_ref[tokens:, :] = (partial - high.astype(jnp.float32)).astype(jnp.bfloat16)


def attention(message, row, tokens, gain, w_qkv, cos, sin, lens, keys, values, w_out):
    loaded = [pltpu.VMEM(a.shape, a.dtype) for a in (w_qkv, keys, values, w_out)]
    return pl.pallas_call(
        functools.partial(attention_kernel, row),
        out_shape=jax.ShapeDtypeStruct((2 * tokens, GROUP * LANES), jnp.bfloat16),
        in_specs=[hbm(), vmem(), hbm(), vmem(), vmem(), vmem(), hbm(), hbm(), hbm()],
        out_specs=vmem(),
        scratch_shapes=[pltpu.VMEM((GROUP, tokens, LANES), jnp.bfloat16)]
        + loaded
        + [pltpu.VMEM((tokens, GROUP * LANES), jnp.bfloat16), pltpu.SemaphoreType.DMA((5,))],
        compiler_params=pltpu.CompilerParams(vmem_limit_bytes=62 << 20),
        cost_estimate=pl.CostEstimate(flops=4 * 10**8, bytes_accessed=9 << 20, transcendentals=40000),
        name="attention",
    )(message, gain, w_qkv, cos, sin, lens, keys, values, w_out)


def combine_kernel(first, base, message_ref, *refs):
    scored, (out_ref, buf, payload, sem) = refs[:-4], refs[-4:]
    tokens = buf.shape[1] // 2
    copy = pltpu.make_async_copy(message_ref.at[:, pl.ds(first, 2 * tokens), :], buf, sem.at[0])
    copy.start()
    payload[tokens:, :] = jnp.zeros((payload.shape[0] - tokens, LANES), jnp.float32)
    for i, part in enumerate(scored):
        at = tokens + i * base
        payload[at : at + part.shape[0], :] = part[...]
    copy.wait()
    total = jnp.zeros((tokens, LANES), jnp.float32)
    for s in range(GROUP):
        total = total + (buf[s, 0:tokens, :].astype(jnp.float32) + buf[s, tokens:, :].astype(jnp.float32))
    payload[0:tokens, :] = total.astype(jnp.bfloat16).astype(jnp.float32)
    for d in range(GROUP):
        pltpu.make_async_copy(payload, out_ref.at[d], sem.at[1]).start()
    pltpu.make_async_copy(out_ref, out_ref, sem.at[1]).wait()


def combine(message, first, base, tokens, scored):
    rows = tokens + 2 * base
    return pl.pallas_call(
        functools.partial(combine_kernel, first, base),
        out_shape=jax.ShapeDtypeStruct((GROUP, rows, LANES), jnp.float32),
        in_specs=[hbm()] + [vmem()] * len(scored),
        out_specs=pl.BlockSpec(memory_space=pltpu.HBM),
        scratch_shapes=[
            pltpu.VMEM((GROUP, 2 * tokens, LANES), jnp.bfloat16),
            pltpu.VMEM((rows, LANES), jnp.float32),
            pltpu.SemaphoreType.DMA((2,)),
        ],
        compiler_params=pltpu.CompilerParams(vmem_limit_bytes=62 << 20),
        cost_estimate=pl.CostEstimate(flops=10**5, bytes_accessed=1 << 19, transcendentals=0),
        name="combine",
    )(message, *scored)


def score_kernel(slots, place_ref, x_hbm, *refs):
    w_hbm, (gain_ref, bias_ref, score_ref, out_ref) = refs[:20], refs[20:24]
    x_buf, w_buf, normed_ref, total_ref, x_sem, w_sems = refs[24:]
    width = GROUP * LANES
    rows = slots * LANES
    x_copy = pltpu.make_async_copy(x_hbm.at[:, pl.ds(0, rows), :], x_buf, x_sem.at[0])
    x_copy.start()
    core, x, z, ylo = place_ref[0], place_ref[1], place_ref[2], place_ref[3]
    for side in range(2):
        owner = core if side == 0 else 1 - core
        near = jnp.where(owner == 0, z, x)
        far = jnp.where(owner == 0, x, z)
        for index, (step, begin, end) in enumerate(RECEIVED + RECEIVED):
            last = (far + step) & 3
            low = ylo if index < len(RECEIVED) else 1 - ylo

            @pl.loop(begin, end)
            def _(a):
                mine = (near + jnp.where(a < 2, -a, a - 1)) & 3
                block = jnp.where(owner == 0, last * 4 + mine, mine * 4 + last) * 2 + low
                pltpu.make_async_copy(
                    w_hbm[side * 10 + index].at[pl.ds(pl.multiple_of((a - begin) * LANES, LANES), LANES), :],
                    w_buf.at[owner, pl.ds(pl.multiple_of(block * LANES, LANES), LANES), :],
                    w_sems.at[owner],
                ).start()

    x_copy.wait()

    @pl.loop(0, slots)
    def _(q):
        here = pl.ds(pl.multiple_of(q * LANES, LANES), LANES)

        def square(c, squares):
            for i in range(CHUNK):
                part = x_buf[c * CHUNK + i, here, :].astype(jnp.float32)
                squares = squares + part * part
            return squares

        squares = lax.fori_loop(0, GROUP // CHUNK, square, jnp.zeros((LANES, LANES), jnp.float32))
        mean = jnp.sum(squares, axis=-1, keepdims=True) / width
        inverse_rms = lax.rsqrt(mean + EPS)

        @pl.loop(0, GROUP // CHUNK)
        def _(c):
            for i in range(CHUNK):
                s = c * CHUNK + i
                part = x_buf[s, here, :].astype(jnp.float32) * inverse_rms * gain_ref[pl.ds(s, 1), :]
                normed_ref[here, pl.ds(pl.multiple_of(s * LANES, LANES), LANES)] = part.astype(jnp.bfloat16)

    total_ref[...] = jnp.zeros_like(total_ref)

    @pl.loop(0, 4)
    def _(i):
        owner = jnp.where(i < 2, core, 1 - core)
        h = i & 1

        @pl.when(h == 0)
        def _():
            pltpu.make_async_copy(w_buf.at[owner], w_buf.at[owner], w_sems.at[owner]).wait()

        bias, score = bias_ref[pl.ds(owner * 2 + h, 1), :], score_ref[pl.ds(owner * 2 + h, 1), :]
        w = w_buf[owner, :, pl.ds(pl.multiple_of(h * COLS, COLS), COLS)]
        for part in range(0, rows, HALF):
            some = slice(part, min(part + HALF, rows))
            pre = jnp.dot(normed_ref[some, :], w, preferred_element_type=jnp.float32) + bias
            hidden = pre / (1.0 + jnp.exp(-pre)) * score
            total = total_ref[some, :]
            for c in range(COLS // LANES):
                total = total + hidden[:, c * LANES : (c + 1) * LANES]
            total_ref[some, :] = total

    for q in range(slots):
        out_ref[q : q + 1, :] = jnp.sum(total_ref[q * LANES : (q + 1) * LANES, :].T, axis=0, keepdims=True)


def score_rows(message, slots, place, parts, gain, bias, w_score):
    width = GROUP * LANES
    rows = slots * LANES
    return pl.pallas_call(
        functools.partial(score_kernel, slots),
        out_shape=jax.ShapeDtypeStruct((slots, LANES), jnp.float32),
        in_specs=[pl.BlockSpec(memory_space=pltpu.SMEM)] + [hbm()] * 21 + [vmem()] * 3,
        out_specs=vmem(),
        scratch_shapes=[
            pltpu.VMEM((GROUP, rows, LANES), jnp.bfloat16),
            pltpu.VMEM((2, width, 2 * COLS), jnp.bfloat16),
            pltpu.VMEM((rows, width), jnp.bfloat16),
            pltpu.VMEM((rows, LANES), jnp.float32),
            pltpu.SemaphoreType.DMA((1,)),
            pltpu.SemaphoreType.DMA((2,)),
        ],
        compiler_params=pltpu.CompilerParams(vmem_limit_bytes=62 << 20),
        cost_estimate=pl.CostEstimate(
            flops=2 * rows * width * 4 * COLS, bytes_accessed=24 << 20, transcendentals=rows * 4 * COLS
        ),
        name="score",
    )(place, message, *parts, gain, bias, w_score)


def block_starts(lens_ref, pieces):
    starts, counts = [], []
    start = 0
    for i in range(pieces):
        count = lax.shift_right_logical(lens_ref[i] + (LANES - 1), 7)
        starts.append(start)
        counts.append(count)
        start = start + count
    return starts, counts


def pack_kernel(pieces, first, slots, lens_ref, pieces_ref, *refs):
    starts, _ = block_starts(lens_ref, pieces)
    blocks = pieces_ref.shape[1] // LANES
    rows = slots * LANES
    if first:
        partial_ref, out_ref, stage, in_sems, out_sem = refs
        extra = partial_ref.shape[0]
    else:
        ids_ref, table_ref, out_ref, stage, tiles, picked, in_sems, out_sem = refs
        tokens = ids_ref.shape[0] * ids_ref.shape[1]
        steps = ids_ref.shape[1]
        for i in range(tokens):
            above = lax.shift_right_logical(ids_ref[i // steps, i % steps], 3) * 8
            pltpu.make_async_copy(table_ref.at[pl.ds(pl.multiple_of(above, 8), 8), :], tiles.at[i], in_sems.at[4]).start()
    chunk = GROUP // 4

    @pl.loop(0, GROUP)
    def _(d):
        sem = in_sems.at[d // chunk]

        @pl.loop(0, slots)
        def _(q):
            slot = (first + q) * GROUP + d
            piece, start = 0, 0
            for i in range(1, pieces):
                after = slot >= starts[i]
                piece = jnp.where(after, i, piece)
                start = jnp.where(after, starts[i], start)
            block = jnp.minimum(slot - start, blocks - 1)
            pltpu.make_async_copy(
                pieces_ref.at[piece, pl.ds(pl.multiple_of(block * LANES, LANES), LANES), :],
                stage.at[d, pl.ds(pl.multiple_of(q * LANES, LANES), LANES), :],
                sem,
            ).start()

        if first:
            source = partial_ref.at[:, pl.ds(pl.multiple_of(d * LANES, LANES), LANES)]
            pltpu.make_async_copy(source, stage.at[d, pl.ds(rows, extra), :], sem).start()

    if not first:
        pltpu.make_async_copy(tiles, tiles, in_sems.at[4]).wait()
        sublane = lax.broadcasted_iota(jnp.int32, (8, LANES), 0)
        for i in range(tokens):
            own = sublane == (ids_ref[i // steps, i % steps] & 7)
            picked[i : i + 1, :] = jnp.sum(jnp.where(own, tiles[i].astype(jnp.float32), 0.0), axis=0, keepdims=True)
        block = picked[...].astype(jnp.bfloat16)
        for d in range(GROUP):
            stage[d, rows:, :] = block
    done = stage.shape[1] if first else rows
    for c in range(4):
        part = pl.ds(c * chunk, chunk)
        landed = stage.at[part, pl.ds(0, done), :]
        pltpu.make_async_copy(landed, landed, in_sems.at[c]).wait()
        pltpu.make_async_copy(stage.at[part], out_ref.at[part], out_sem.at[c]).start()
    for c in range(4):
        part = pl.ds(c * chunk, chunk)
        pltpu.make_async_copy(stage.at[part], out_ref.at[part], out_sem.at[c]).wait()


def pack(first, slots, extra, scratch, operands, specs):
    rows = slots * LANES + extra
    return pl.pallas_call(
        functools.partial(pack_kernel, operands[1].shape[0], first, slots),
        out_shape=jax.ShapeDtypeStruct((GROUP, rows, LANES), jnp.bfloat16),
        in_specs=[pl.BlockSpec(memory_space=pltpu.SMEM), hbm()] + specs,
        out_specs=pl.BlockSpec(memory_space=pltpu.HBM),
        scratch_shapes=[pltpu.VMEM((GROUP, rows, LANES), jnp.bfloat16)]
        + scratch
        + [pltpu.SemaphoreType.DMA((5,)), pltpu.SemaphoreType.DMA((4,))],
        compiler_params=pltpu.CompilerParams(vmem_limit_bytes=62 << 20),
        cost_estimate=pl.CostEstimate(flops=0, bytes_accessed=4 * GROUP * rows * LANES, transcendentals=0),
    )(*operands)


def pack_first(slots, piece_lens, pieces, step_ids, embed_table):
    tokens = step_ids.shape[0] * step_ids.shape[1]
    scratch = [pltpu.VMEM((tokens, 8, LANES), jnp.bfloat16), pltpu.VMEM((tokens, LANES), jnp.float32)]
    specs = [pl.BlockSpec(memory_space=pltpu.SMEM), hbm()]
    return pack(0, slots, tokens, scratch, (piece_lens, pieces, step_ids, embed_table), specs)


def pack_rest(first, slots, piece_lens, pieces, partial):
    return pack(first, slots, partial.shape[0], [], (piece_lens, pieces, partial), [hbm()])


def finish_kernel(pieces, tokens, scalars_ref, offset_ref, result_ref, attn_ref, value_ref):
    starts, counts = block_starts(scalars_ref, pieces)
    me = scalars_ref[pieces]
    where = me * LANES + lax.broadcasted_iota(jnp.int32, (1, LANES), 1)
    for i in range(pieces):
        slot = jnp.minimum(starts[i] + jnp.minimum(me, counts[i]), pieces * GROUP - 1)
        row = result_ref[slot & (GROUP - 1), pl.ds(tokens + lax.shift_right_logical(slot, 5), 1), :]
        value_ref[i : i + 1, :] = jnp.where(where < scalars_ref[i], row + offset_ref[0], 0.0)
    rows, steps, _ = attn_ref.shape
    for s in range(GROUP):
        block = result_ref[s, 0:tokens, :].reshape(rows, steps, LANES)
        attn_ref[:, :, s * LANES : (s + 1) * LANES] = block.astype(jnp.bfloat16)


def finish(scalars, offset, result, pieces, rows, steps):
    tokens = rows * steps
    return pl.pallas_call(
        functools.partial(finish_kernel, pieces, tokens),
        out_shape=(
            jax.ShapeDtypeStruct((rows, steps, GROUP * LANES), jnp.bfloat16),
            jax.ShapeDtypeStruct((pieces, LANES), jnp.float32),
        ),
        in_specs=[pl.BlockSpec(memory_space=pltpu.SMEM)] * 2 + [vmem()],
        out_specs=(vmem(), vmem()),
        compiler_params=pltpu.CompilerParams(vmem_limit_bytes=16 << 20),
        name="finish",
    )(scalars, offset, result)


def exchange(message):
    return lax.all_to_all(message, MP, 0, 0)


def shift(value, stage, step):
    pairs = []
    for core in range(2):
        for x in range(4):
            for z in range(4):
                along_x = core != stage
                to = ((x + step) % 4 if along_x else x) * 4 + (z if along_x else (z + step) % 4)
                pairs.append((core * 16 + x * 4 + z, core * 16 + to))
    return lax.ppermute(value, ("core", "x", "z"), pairs)


def around(value, stage):
    half = value.shape[0] // 2
    right, left = shift(value, stage, 1), shift(value, stage, -1)
    return (value, right, left, shift(right[:half], stage, 1), shift(left[half:], stage, -1))


def across(value, pairs):
    return lax.ppermute(value, ("yhi", "ylo"), [pair for i, j in pairs for pair in ((i, j), (j, i))])


def gather_layer(w_value, message, most):
    columns = w_value.shape[1] // 2
    own = lax.dynamic_slice_in_dim(w_value, lax.axis_index("core") * columns, columns, axis=1)
    plane = jnp.concatenate(around(own, 0), axis=0)
    half = plane.shape[0] // 2
    right, left = shift(plane, 1, 1), shift(plane, 1, -1)
    ahead, behind, message, most = lax.optimization_barrier((right[:half], left[half:], message, most))
    near = (plane, right, left)
    ahead = shift(ahead, 1, 1)
    behind = shift(behind, 1, -1)
    rest = (ahead, behind)
    outer, inner = ((1, 2), (3, 0)), ((0, 1), (2, 3))
    others = (across(plane, inner),)
    others += (across(right, outer),)
    others += (across(left, outer),) + tuple(across(v, outer) for v in rest)
    return near + rest + others, message, most


def swap_cores(value):
    return lax.ppermute(value, "core", [(0, 1), (1, 0)])


def per_device(
    step_ids,
    prompt_lens,
    embed_table,
    attn_gain,
    w_qkv,
    w_out,
    key_cache,
    value_cache,
    reward_pieces,
    piece_lens,
    reward_gain,
    w_value,
    b_value,
    w_score,
    b_score,
):
    rows, steps = step_ids.shape
    tokens = rows * steps
    me = lax.axis_index(MP)
    place = jnp.stack([lax.axis_index(name) for name in ("core", "x", "z", "ylo")]).astype(jnp.int32)
    bias = b_value.reshape(4, COLS)
    score = w_score.reshape(4, COLS)

    half_dim = LANES // 2
    frequency = 10000.0 ** (-2.0 * jnp.arange(half_dim, dtype=jnp.float32) / (2 * half_dim))
    positions = (prompt_lens[:, None] + jnp.arange(steps, dtype=jnp.int32)[None, :]).reshape(tokens)
    angles = positions.astype(jnp.float32)[:, None] * frequency
    cos = jnp.concatenate([jnp.cos(angles)] * 2, axis=-1)
    sin = jnp.concatenate([-jnp.sin(angles), jnp.sin(angles)], axis=-1)
    lens = jnp.broadcast_to(jnp.repeat(prompt_lens, steps)[:, None], (tokens, LANES))
    pieces, length, _ = reward_pieces.shape
    total = jnp.sum((piece_lens + (LANES - 1)) // LANES)
    most = jnp.full((8, LANES), total, jnp.int32).astype(jnp.float32)
    for axis in ("core", "yhi"):
        most = jnp.maximum(most, lax.ppermute(most, axis, [(0, 1), (1, 0)]))
    base = length // LANES * pieces // GROUP // 2
    message = pack_first(base, piece_lens, reward_pieces, step_ids, embed_table)
    parts, message, most = gather_layer(w_value, message, most)
    rest = jnp.clip((most[0, 0].astype(jnp.int32) + (GROUP - 1)) // GROUP - base, 0, base)
    first = exchange(message)
    partial = attention(
        first,
        base * LANES,
        tokens,
        attn_gain.astype(jnp.float32).reshape(GROUP, LANES),
        w_qkv,
        cos,
        sin,
        lens,
        key_cache.reshape(rows, -1, LANES),
        value_cache.reshape(rows, -1, LANES),
        w_out,
    )
    gain = reward_gain.astype(jnp.float32).reshape(GROUP, LANES)
    swapped = tuple(swap_cores(part) for part in parts[:-2])
    *last, partial = lax.optimization_barrier(parts[-2:] + (partial,))
    parts = parts + swapped + tuple(swap_cores(part) for part in last)

    def remainder(slots, first, partial, place, piece_lens, reward_pieces, gain, bias, score, parts):
        second = exchange(pack_rest(base, slots, piece_lens, reward_pieces, partial))
        scored = [score_rows(first, base, place, parts, gain, bias, score)]
        if slots:
            scored.append(score_rows(second, slots, place, parts, gain, bias, score))
        return combine(second, slots * LANES, base, tokens, scored)

    payload = lax.switch(
        rest,
        [functools.partial(remainder, slots) for slots in range(base + 1)],
        first,
        partial,
        place,
        piece_lens,
        reward_pieces,
        gain,
        bias,
        score,
        parts,
    )
    scalars = jnp.concatenate([piece_lens, me.reshape(1).astype(jnp.int32)])
    attn_out, piece_values = finish(scalars, b_score, exchange(payload), pieces, rows, steps)
    return (attn_out, piece_values)


def solution(mesh):
    fine = Mesh(mesh.devices.reshape(2, 2, 4, 4, 2), DP + MP)
    return jax.shard_map(
        per_device,
        mesh=fine,
        in_specs=(
            P(DP, None),
            P(DP),
            P(None, MP),
            P(),
            P(None, None, MP),
            P(MP, None),
            P(DP, MP, None, None),
            P(DP, MP, None, None),
            P(DP, None, MP),
            P(DP),
            P(),
            P(MP, None),
            P(),
            P(),
            P(),
        ),
        out_specs=(P(DP, None, None), P(DP, MP)),
        check_vma=False,
    )
```

```python
import functools
import math

import jax
import jax.numpy as jnp
from jax import lax
from jax.experimental import pallas as pl
from jax.experimental.pallas import tpu as pltpu
from jax.sharding import Mesh, PartitionSpec as P


EPS = 1e-05
MASKED = -1e30
DP = ("yhi", "core")
MP = ("x", "z", "ylo")
GROUP = 32
LANES = 128
COLS = 512
HALF = 256
CHUNK = 4
RECEIVED = ((0, 0, 4), (-1, 0, 4), (1, 0, 4), (2, 0, 2), (2, 2, 4))


def vmem():
    return pl.BlockSpec(memory_space=pltpu.VMEM)


def hbm():
    return pl.BlockSpec(memory_space=pl.ANY)


def attention_kernel(row, message_ref, gain_ref, wqkv_hbm, cos_ref, sin_ref, lens_ref, key_hbm, value_hbm, wout_hbm, out_ref, *scratch):
    emb_ref, wqkv_ref, key_ref, value_ref, wout_ref, normed_ref, sems = scratch
    tokens = emb_ref.shape[1]
    copies = [
        pltpu.make_async_copy(source, target, sems.at[i])
        for i, (source, target) in enumerate(
            [
                (message_ref.at[:, pl.ds(row, tokens), :], emb_ref),
                (wqkv_hbm, wqkv_ref),
                (key_hbm, key_ref),
                (value_hbm, value_ref),
                (wout_hbm, wout_ref),
            ]
        )
    ]
    for copy in copies:
        copy.start()
    width = GROUP * LANES
    rows = key_ref.shape[0]
    steps = tokens // rows
    copies[0].wait()
    squares = jnp.zeros((tokens, LANES), jnp.float32)
    for s in range(GROUP):
        part = emb_ref[s].astype(jnp.float32)
        squares = squares + part * part
    mean = jnp.sum(squares, axis=-1, keepdims=True) / width
    inverse_rms = lax.rsqrt(mean + EPS)
    for s in range(GROUP):
        part = emb_ref[s].astype(jnp.float32) * inverse_rms * gain_ref[s : s + 1, :]
        normed_ref[:, s * LANES : (s + 1) * LANES] = part.astype(jnp.bfloat16)
    normed = normed_ref[...]
    copies[1].wait()
    parts = [jnp.dot(normed, wqkv_ref[c], preferred_element_type=jnp.float32) for c in range(3)]
    cos, sin = cos_ref[...], sin_ref[...]
    half = LANES // 2

    def rotate(v):
        return (v * cos + pltpu.roll(v, half, 1) * sin).astype(jnp.bfloat16)

    queries, new_keys = rotate(parts[0]), rotate(parts[1])
    new_values = parts[2].astype(jnp.bfloat16)
    root = 1.0 / math.sqrt(LANES)
    slots = key_ref.shape[1]
    group_of = lax.broadcasted_iota(jnp.int32, (tokens, slots), 0) // steps
    scores = jnp.zeros((tokens, slots), jnp.float32)
    copies[2].wait()
    for r in range(rows):
        one = lax.dot_general(queries, key_ref[r], (((1,), (1,)), ((), ())), preferred_element_type=jnp.float32)
        scores = jnp.where(group_of == r, one, scores)
    live = lax.broadcasted_iota(jnp.int32, (tokens, slots), 1) < lens_ref[:, 0:1]
    scores = jnp.where(live, scores * root, MASKED)
    fresh = lax.dot_general(queries, new_keys, (((1,), (1,)), ((), ())), preferred_element_type=jnp.float32)
    i = lax.broadcasted_iota(jnp.int32, (tokens, tokens), 0)
    j = lax.broadcasted_iota(jnp.int32, (tokens, tokens), 1)
    causal = (i // steps == j // steps) & (j <= i)
    fresh = jnp.where(causal, fresh * root, MASKED)
    top = jnp.maximum(jnp.max(scores, axis=-1, keepdims=True), jnp.max(fresh, axis=-1, keepdims=True))
    weights = jnp.exp(scores - top)
    fresh_weights = jnp.exp(fresh - top)
    total = jnp.sum(weights, axis=-1, keepdims=True) + jnp.sum(fresh_weights, axis=-1, keepdims=True)
    mixed = jnp.dot(fresh_weights.astype(jnp.bfloat16), new_values, preferred_element_type=jnp.float32)
    copies[3].wait()
    for r in range(rows):
        own = jnp.where(group_of == r, weights, 0.0).astype(jnp.bfloat16)
        mixed = mixed + jnp.dot(own, value_ref[r], preferred_element_type=jnp.float32)
    heads = (mixed / total).astype(jnp.bfloat16)
    copies[4].wait()
    partial = jnp.dot(heads, wout_ref[...], preferred_element_type=jnp.float32)
    high = partial.astype(jnp.bfloat16)
    out_ref[0:tokens, :] = high
    out_ref[tokens:, :] = (partial - high.astype(jnp.float32)).astype(jnp.bfloat16)


def attention(message, row, tokens, gain, w_qkv, cos, sin, lens, keys, values, w_out):
    loaded = [pltpu.VMEM(a.shape, a.dtype) for a in (w_qkv, keys, values, w_out)]
    return pl.pallas_call(
        functools.partial(attention_kernel, row),
        out_shape=jax.ShapeDtypeStruct((2 * tokens, GROUP * LANES), jnp.bfloat16),
        in_specs=[hbm(), vmem(), hbm(), vmem(), vmem(), vmem(), hbm(), hbm(), hbm()],
        out_specs=vmem(),
        scratch_shapes=[pltpu.VMEM((GROUP, tokens, LANES), jnp.bfloat16)]
        + loaded
        + [pltpu.VMEM((tokens, GROUP * LANES), jnp.bfloat16), pltpu.SemaphoreType.DMA((5,))],
        compiler_params=pltpu.CompilerParams(vmem_limit_bytes=62 << 20),
        cost_estimate=pl.CostEstimate(flops=4 * 10**8, bytes_accessed=9 << 20, transcendentals=40000),
        name="attention",
    )(message, gain, w_qkv, cos, sin, lens, keys, values, w_out)


def combine_kernel(first, base, message_ref, *refs):
    scored, (out_ref, buf, payload, sem) = refs[:-4], refs[-4:]
    tokens = buf.shape[1] // 2
    copy = pltpu.make_async_copy(message_ref.at[:, pl.ds(first, 2 * tokens), :], buf, sem.at[0])
    copy.start()
    payload[tokens:, :] = jnp.zeros((payload.shape[0] - tokens, LANES), jnp.float32)
    for i, part in enumerate(scored):
        at = tokens + i * base
        payload[at : at + part.shape[0], :] = part[...]
    copy.wait()
    total = jnp.zeros((tokens, LANES), jnp.float32)
    for s in range(GROUP):
        total = total + (buf[s, 0:tokens, :].astype(jnp.float32) + buf[s, tokens:, :].astype(jnp.float32))
    payload[0:tokens, :] = total.astype(jnp.bfloat16).astype(jnp.float32)
    for d in range(GROUP):
        pltpu.make_async_copy(payload, out_ref.at[d], sem.at[1]).start()
    pltpu.make_async_copy(out_ref, out_ref, sem.at[1]).wait()


def combine(message, first, base, tokens, scored):
    rows = tokens + 2 * base
    return pl.pallas_call(
        functools.partial(combine_kernel, first, base),
        out_shape=jax.ShapeDtypeStruct((GROUP, rows, LANES), jnp.float32),
        in_specs=[hbm()] + [vmem()] * len(scored),
        out_specs=pl.BlockSpec(memory_space=pltpu.HBM),
        scratch_shapes=[
            pltpu.VMEM((GROUP, 2 * tokens, LANES), jnp.bfloat16),
            pltpu.VMEM((rows, LANES), jnp.float32),
            pltpu.SemaphoreType.DMA((2,)),
        ],
        compiler_params=pltpu.CompilerParams(vmem_limit_bytes=62 << 20),
        cost_estimate=pl.CostEstimate(flops=10**5, bytes_accessed=1 << 19, transcendentals=0),
        name="combine",
    )(message, *scored)


def score_kernel(slots, place_ref, x_hbm, *refs):
    w_hbm, (gain_ref, bias_ref, score_ref, out_ref) = refs[:20], refs[20:24]
    x_buf, w_buf, normed_ref, total_ref, x_sem, w_sems = refs[24:]
    width = GROUP * LANES
    rows = slots * LANES
    x_copy = pltpu.make_async_copy(x_hbm.at[:, pl.ds(0, rows), :], x_buf, x_sem.at[0])
    x_copy.start()
    core, x, z, ylo = place_ref[0], place_ref[1], place_ref[2], place_ref[3]
    for side in range(2):
        owner = core if side == 0 else 1 - core
        near = jnp.where(owner == 0, z, x)
        far = jnp.where(owner == 0, x, z)
        for index, (step, begin, end) in enumerate(RECEIVED + RECEIVED):
            last = (far + step) & 3
            low = ylo if index < len(RECEIVED) else 1 - ylo

            @pl.loop(begin, end)
            def _(a):
                mine = (near + jnp.where(a < 2, -a, a - 1)) & 3
                block = jnp.where(owner == 0, last * 4 + mine, mine * 4 + last) * 2 + low
                pltpu.make_async_copy(
                    w_hbm[side * 10 + index].at[pl.ds(pl.multiple_of((a - begin) * LANES, LANES), LANES), :],
                    w_buf.at[owner, pl.ds(pl.multiple_of(block * LANES, LANES), LANES), :],
                    w_sems.at[owner],
                ).start()

    x_copy.wait()

    @pl.loop(0, slots)
    def _(q):
        here = pl.ds(pl.multiple_of(q * LANES, LANES), LANES)

        def square(c, squares):
            for i in range(CHUNK):
                part = x_buf[c * CHUNK + i, here, :].astype(jnp.float32)
                squares = squares + part * part
            return squares

        squares = lax.fori_loop(0, GROUP // CHUNK, square, jnp.zeros((LANES, LANES), jnp.float32))
        mean = jnp.sum(squares, axis=-1, keepdims=True) / width
        inverse_rms = lax.rsqrt(mean + EPS)

        @pl.loop(0, GROUP // CHUNK)
        def _(c):
            for i in range(CHUNK):
                s = c * CHUNK + i
                part = x_buf[s, here, :].astype(jnp.float32) * inverse_rms * gain_ref[pl.ds(s, 1), :]
                normed_ref[here, pl.ds(pl.multiple_of(s * LANES, LANES), LANES)] = part.astype(jnp.bfloat16)

    total_ref[...] = jnp.zeros_like(total_ref)

    @pl.loop(0, 4)
    def _(i):
        owner = jnp.where(i < 2, core, 1 - core)
        h = i & 1

        @pl.when(h == 0)
        def _():
            pltpu.make_async_copy(w_buf.at[owner], w_buf.at[owner], w_sems.at[owner]).wait()

        bias, score = bias_ref[pl.ds(owner * 2 + h, 1), :], score_ref[pl.ds(owner * 2 + h, 1), :]
        w = w_buf[owner, :, pl.ds(pl.multiple_of(h * COLS, COLS), COLS)]
        for part in range(0, rows, HALF):
            some = slice(part, min(part + HALF, rows))
            pre = jnp.dot(normed_ref[some, :], w, preferred_element_type=jnp.float32) + bias
            hidden = pre / (1.0 + jnp.exp(-pre)) * score
            total = total_ref[some, :]
            for c in range(COLS // LANES):
                total = total + hidden[:, c * LANES : (c + 1) * LANES]
            total_ref[some, :] = total

    for q in range(slots):
        out_ref[q : q + 1, :] = jnp.sum(total_ref[q * LANES : (q + 1) * LANES, :].T, axis=0, keepdims=True)


def score_rows(message, slots, place, parts, gain, bias, w_score):
    width = GROUP * LANES
    rows = slots * LANES
    return pl.pallas_call(
        functools.partial(score_kernel, slots),
        out_shape=jax.ShapeDtypeStruct((slots, LANES), jnp.float32),
        in_specs=[pl.BlockSpec(memory_space=pltpu.SMEM)] + [hbm()] * 21 + [vmem()] * 3,
        out_specs=vmem(),
        scratch_shapes=[
            pltpu.VMEM((GROUP, rows, LANES), jnp.bfloat16),
            pltpu.VMEM((2, width, 2 * COLS), jnp.bfloat16),
            pltpu.VMEM((rows, width), jnp.bfloat16),
            pltpu.VMEM((rows, LANES), jnp.float32),
            pltpu.SemaphoreType.DMA((1,)),
            pltpu.SemaphoreType.DMA((2,)),
        ],
        compiler_params=pltpu.CompilerParams(vmem_limit_bytes=62 << 20),
        cost_estimate=pl.CostEstimate(
            flops=2 * rows * width * 4 * COLS, bytes_accessed=24 << 20, transcendentals=rows * 4 * COLS
        ),
        name="score",
    )(place, message, *parts, gain, bias, w_score)


def block_starts(lens_ref, pieces):
    starts, counts = [], []
    start = 0
    for i in range(pieces):
        count = lax.shift_right_logical(lens_ref[i] + (LANES - 1), 7)
        starts.append(start)
        counts.append(count)
        start = start + count
    return starts, counts


def pack_kernel(pieces, first, slots, lens_ref, pieces_ref, *refs):
    starts, _ = block_starts(lens_ref, pieces)
    blocks = pieces_ref.shape[1] // LANES
    rows = slots * LANES
    if first:
        partial_ref, out_ref, stage, in_sems, out_sem = refs
        extra = partial_ref.shape[0]
    else:
        ids_ref, table_ref, out_ref, stage, tiles, picked, in_sems, out_sem = refs
        tokens = ids_ref.shape[0] * ids_ref.shape[1]
        steps = ids_ref.shape[1]
        for i in range(tokens):
            above = lax.shift_right_logical(ids_ref[i // steps, i % steps], 3) * 8
            pltpu.make_async_copy(table_ref.at[pl.ds(pl.multiple_of(above, 8), 8), :], tiles.at[i], in_sems.at[4]).start()
    chunk = GROUP // 4

    @pl.loop(0, GROUP)
    def _(d):
        sem = in_sems.at[d // chunk]

        @pl.loop(0, slots)
        def _(q):
            slot = (first + q) * GROUP + d
            piece, start = 0, 0
            for i in range(1, pieces):
                after = slot >= starts[i]
                piece = jnp.where(after, i, piece)
                start = jnp.where(after, starts[i], start)
            block = jnp.minimum(slot - start, blocks - 1)
            pltpu.make_async_copy(
                pieces_ref.at[piece, pl.ds(pl.multiple_of(block * LANES, LANES), LANES), :],
                stage.at[d, pl.ds(pl.multiple_of(q * LANES, LANES), LANES), :],
                sem,
            ).start()

        if first:
            source = partial_ref.at[:, pl.ds(pl.multiple_of(d * LANES, LANES), LANES)]
            pltpu.make_async_copy(source, stage.at[d, pl.ds(rows, extra), :], sem).start()

    if not first:
        pltpu.make_async_copy(tiles, tiles, in_sems.at[4]).wait()
        sublane = lax.broadcasted_iota(jnp.int32, (8, LANES), 0)
        for i in range(tokens):
            own = sublane == (ids_ref[i // steps, i % steps] & 7)
            picked[i : i + 1, :] = jnp.sum(jnp.where(own, tiles[i].astype(jnp.float32), 0.0), axis=0, keepdims=True)
        block = picked[...].astype(jnp.bfloat16)
        for d in range(GROUP):
            stage[d, rows:, :] = block
    done = stage.shape[1] if first else rows
    for c in range(4):
        part = pl.ds(c * chunk, chunk)
        landed = stage.at[part, pl.ds(0, done), :]
        pltpu.make_async_copy(landed, landed, in_sems.at[c]).wait()
        pltpu.make_async_copy(stage.at[part], out_ref.at[part], out_sem.at[c]).start()
    for c in range(4):
        part = pl.ds(c * chunk, chunk)
        pltpu.make_async_copy(stage.at[part], out_ref.at[part], out_sem.at[c]).wait()


def pack(first, slots, extra, scratch, operands, specs):
    rows = slots * LANES + extra
    return pl.pallas_call(
        functools.partial(pack_kernel, operands[1].shape[0], first, slots),
        out_shape=jax.ShapeDtypeStruct((GROUP, rows, LANES), jnp.bfloat16),
        in_specs=[pl.BlockSpec(memory_space=pltpu.SMEM), hbm()] + specs,
        out_specs=pl.BlockSpec(memory_space=pltpu.HBM),
        scratch_shapes=[pltpu.VMEM((GROUP, rows, LANES), jnp.bfloat16)]
        + scratch
        + [pltpu.SemaphoreType.DMA((5,)), pltpu.SemaphoreType.DMA((4,))],
        compiler_params=pltpu.CompilerParams(vmem_limit_bytes=62 << 20),
        cost_estimate=pl.CostEstimate(flops=0, bytes_accessed=4 * GROUP * rows * LANES, transcendentals=0),
    )(*operands)


def pack_first(slots, piece_lens, pieces, step_ids, embed_table):
    tokens = step_ids.shape[0] * step_ids.shape[1]
    scratch = [pltpu.VMEM((tokens, 8, LANES), jnp.bfloat16), pltpu.VMEM((tokens, LANES), jnp.float32)]
    specs = [pl.BlockSpec(memory_space=pltpu.SMEM), hbm()]
    return pack(0, slots, tokens, scratch, (piece_lens, pieces, step_ids, embed_table), specs)


def pack_rest(first, slots, piece_lens, pieces, partial):
    return pack(first, slots, partial.shape[0], [], (piece_lens, pieces, partial), [hbm()])


def finish_kernel(pieces, tokens, scalars_ref, offset_ref, result_ref, attn_ref, value_ref):
    starts, counts = block_starts(scalars_ref, pieces)
    me = scalars_ref[pieces]
    where = me * LANES + lax.broadcasted_iota(jnp.int32, (1, LANES), 1)
    for i in range(pieces):
        slot = jnp.minimum(starts[i] + jnp.minimum(me, counts[i]), pieces * GROUP - 1)
        row = result_ref[slot & (GROUP - 1), pl.ds(tokens + lax.shift_right_logical(slot, 5), 1), :]
        value_ref[i : i + 1, :] = jnp.where(where < scalars_ref[i], row + offset_ref[0], 0.0)
    rows, steps, _ = attn_ref.shape
    for s in range(GROUP):
        block = result_ref[s, 0:tokens, :].reshape(rows, steps, LANES)
        attn_ref[:, :, s * LANES : (s + 1) * LANES] = block.astype(jnp.bfloat16)


def finish(scalars, offset, result, pieces, rows, steps):
    tokens = rows * steps
    return pl.pallas_call(
        functools.partial(finish_kernel, pieces, tokens),
        out_shape=(
            jax.ShapeDtypeStruct((rows, steps, GROUP * LANES), jnp.bfloat16),
            jax.ShapeDtypeStruct((pieces, LANES), jnp.float32),
        ),
        in_specs=[pl.BlockSpec(memory_space=pltpu.SMEM)] * 2 + [vmem()],
        out_specs=(vmem(), vmem()),
        compiler_params=pltpu.CompilerParams(vmem_limit_bytes=16 << 20),
        name="finish",
    )(scalars, offset, result)


def exchange(message):
    return lax.all_to_all(message, MP, 0, 0)


def shift(value, stage, step):
    pairs = []
    for core in range(2):
        for x in range(4):
            for z in range(4):
                along_x = core != stage
                to = ((x + step) % 4 if along_x else x) * 4 + (z if along_x else (z + step) % 4)
                pairs.append((core * 16 + x * 4 + z, core * 16 + to))
    return lax.ppermute(value, ("core", "x", "z"), pairs)


def around(value, stage):
    half = value.shape[0] // 2
    right = shift(value, stage, 1)
    left = shift(value, stage, -1)
    ahead = shift(right[:half], stage, 1)
    return (value, right, left, ahead, shift(left[half:], stage, -1))


def across(value, pairs):
    return lax.ppermute(value, ("yhi", "ylo"), [pair for i, j in pairs for pair in ((i, j), (j, i))])


def gather_layer(w_value, message, most):
    columns = w_value.shape[1] // 2
    own = lax.dynamic_slice_in_dim(w_value, lax.axis_index("core") * columns, columns, axis=1)
    plane = jnp.concatenate(around(own, 0), axis=0)
    half = plane.shape[0] // 2
    right = shift(plane, 1, 1)
    left = shift(plane, 1, -1)
    ahead, behind, message, most = lax.optimization_barrier((right[:half], left[half:], message, most))
    near = (plane, right, left)
    ahead = shift(ahead, 1, 1)
    behind = shift(behind, 1, -1)
    rest = (ahead, behind)
    outer, inner = ((1, 2), (3, 0)), ((0, 1), (2, 3))
    others = (across(plane, inner),)
    others += (across(right, outer),)
    others += (across(left, outer),) + tuple(across(v, outer) for v in rest)
    return near + rest + others, message, most


def swap_cores(value):
    return lax.ppermute(value, "core", [(0, 1), (1, 0)])


def per_device(
    step_ids,
    prompt_lens,
    embed_table,
    attn_gain,
    w_qkv,
    w_out,
    key_cache,
    value_cache,
    reward_pieces,
    piece_lens,
    reward_gain,
    w_value,
    b_value,
    w_score,
    b_score,
):
    rows, steps = step_ids.shape
    tokens = rows * steps
    me = lax.axis_index(MP)
    place = jnp.stack([lax.axis_index(name) for name in ("core", "x", "z", "ylo")]).astype(jnp.int32)
    bias = b_value.reshape(4, COLS)
    score = w_score.reshape(4, COLS)

    half_dim = LANES // 2
    frequency = 10000.0 ** (-2.0 * jnp.arange(half_dim, dtype=jnp.float32) / (2 * half_dim))
    positions = (prompt_lens[:, None] + jnp.arange(steps, dtype=jnp.int32)[None, :]).reshape(tokens)
    angles = positions.astype(jnp.float32)[:, None] * frequency
    cos = jnp.concatenate([jnp.cos(angles)] * 2, axis=-1)
    sin = jnp.concatenate([-jnp.sin(angles), jnp.sin(angles)], axis=-1)
    lens = jnp.broadcast_to(jnp.repeat(prompt_lens, steps)[:, None], (tokens, LANES))
    pieces, length, _ = reward_pieces.shape
    total = jnp.sum((piece_lens + (LANES - 1)) // LANES)
    most = jnp.full((8, LANES), total, jnp.int32).astype(jnp.float32)
    for axis in ("core", "yhi"):
        most = jnp.maximum(most, lax.ppermute(most, axis, [(0, 1), (1, 0)]))
    base = length // LANES * pieces // GROUP // 2
    message = pack_first(base, piece_lens, reward_pieces, step_ids, embed_table)
    parts, message, most = gather_layer(w_value, message, most)
    rest = jnp.clip((most[0, 0].astype(jnp.int32) + (GROUP - 1)) // GROUP - base, 0, base)
    first = exchange(message)
    partial = attention(
        first,
        base * LANES,
        tokens,
        attn_gain.astype(jnp.float32).reshape(GROUP, LANES),
        w_qkv,
        cos,
        sin,
        lens,
        key_cache.reshape(rows, -1, LANES),
        value_cache.reshape(rows, -1, LANES),
        w_out,
    )
    gain = reward_gain.astype(jnp.float32).reshape(GROUP, LANES)
    swapped = tuple(swap_cores(part) for part in parts[:-2])
    *last, partial = lax.optimization_barrier(parts[-2:] + (partial,))
    parts = parts + swapped + tuple(swap_cores(part) for part in last)

    def remainder(slots, first, partial, place, piece_lens, reward_pieces, gain, bias, score, parts):
        second = exchange(pack_rest(base, slots, piece_lens, reward_pieces, partial))
        scored = [score_rows(first, base, place, parts, gain, bias, score)]
        if slots:
            scored.append(score_rows(second, slots, place, parts, gain, bias, score))
        return combine(second, slots * LANES, base, tokens, scored)

    payload = lax.switch(
        rest,
        [functools.partial(remainder, slots) for slots in range(base + 1)],
        first,
        partial,
        place,
        piece_lens,
        reward_pieces,
        gain,
        bias,
        score,
        parts,
    )
    scalars = jnp.concatenate([piece_lens, me.reshape(1).astype(jnp.int32)])
    attn_out, piece_values = finish(scalars, b_score, exchange(payload), pieces, rows, steps)
    return (attn_out, piece_values)


def solution(mesh):
    fine = Mesh(mesh.devices.reshape(2, 2, 4, 4, 2), DP + MP)
    return jax.shard_map(
        per_device,
        mesh=fine,
        in_specs=(
            P(DP, None),
            P(DP),
            P(None, MP),
            P(),
            P(None, None, MP),
            P(MP, None),
            P(DP, MP, None, None),
            P(DP, MP, None, None),
            P(DP, None, MP),
            P(DP),
            P(),
            P(MP, None),
            P(),
            P(),
            P(),
        ),
        out_specs=(P(DP, None, None), P(DP, MP)),
        check_vma=False,
    )
```
